32 devices in a mesh: dp: 8 (over z, x), shard: 4 (over y, core).
Axes of the slice: x: 2, y: 2, z: 4, core: 2. Of those that a mesh axis runs over, the one named last changes fastest.
Arguments:
- tokens: bfloat16 [256, 28, 28, 384], P(('dp', 'shard')), may hold values from -6 to 6
- crop_ids: int32 [256, 28, 28], P(('dp', 'shard')), may hold values from 0 to 783, as said below
- params: float32 [1774080], P(('dp', 'shard')), may hold values from -1 to 2
- first_moment: float32 [1774080], P(('dp', 'shard')), may hold values from -1 to 1
- second_moment: float32 [1774080], P(('dp', 'shard')), may hold values from 0 to 1, as said below
- bias_table: float32 [169, 12], replicated, may hold values from -4 to 4
- table_first: float32 [169, 12], replicated, may hold values from -0.005859375 to 0.005859375
- table_second: float32 [169, 12], replicated, may hold values from 3.378173e-10 to 1.3512692e-09
- cotangent: bfloat16 [256, 28, 28, 384], P(('dp', 'shard')), may hold values from -6 to 6
Outputs:
- out_tokens: bfloat16 [256, 28, 28, 384], P(('dp', 'shard'))
- grad_tokens: float32 [256, 28, 28, 384], P(('dp', 'shard'))
- param_grad: float32 [1774080], P(('dp', 'shard'))
- table_grad: float32 [169, 12], replicated
- grad_norm: float32 [], replicated
- new_params: float32 [1774080], P(('dp', 'shard'))
- new_first: float32 [1774080], P(('dp', 'shard'))
- new_second: float32 [1774080], P(('dp', 'shard'))
- new_table: float32 [169, 12], replicated
- new_table_first: float32 [169, 12], replicated
- new_table_second: float32 [169, 12], replicated
The draws below stay inside these ranges and needn't reach their ends.
Inputs may be any that keep to these rules, and one draw needn't show every extreme that they name: `crop_ids`: cells of a canvas with equal ids form one rectangle (a crop). `second_moment`: Positive.
All inputs are finite; a program needn't handle non-finite values.
Results may differ from the reference program's by a relative error of at most 0.012.
Values may be sent and summed in bfloat16 or wider, within the bound.
A program may use at most 384 MiB of HBM per device.

```python
import math
import jax
import jax.numpy as jnp
from jax import lax

D = 384
HEADS = 12
HDIM = 32
FF = 1536
WIN = 7
SHIFT = 3
STEP = 10
ROWS = 28
COLS = 28
NCANV = 256
TABLE = 169
P_SIZE = 1774080


def draw_crop_ids(key, part):
    row_key = jax.random.fold_in(key, 11)
    col_key = jax.random.fold_in(key, 12)
    row_index = jnp.arange(ROWS, dtype=jnp.int32)
    col_index = jnp.arange(COLS, dtype=jnp.int32)
    row_random = jax.random.randint(row_key, (NCANV, ROWS), 0, 6) == 0
    row_starts = jnp.logical_or(row_random, jnp.logical_or(row_index[None, :] == 0, row_index[None, :] == ROWS - 1))
    band_start = lax.cummax(jnp.where(row_starts, row_index[None, :], 0).astype(jnp.int32), axis=1)
    col_random = jax.random.randint(col_key, (NCANV, ROWS, COLS), 0, 7) == 0
    col_starts = jnp.logical_or(col_random, jnp.logical_or(col_index[None, None, :] == 0, col_index[None, None, :] == COLS - 1))
    segment_start = lax.cummax(jnp.where(col_starts, col_index[None, None, :], 0).astype(jnp.int32), axis=2)
    band_full = jnp.broadcast_to(band_start[:, :, None], (NCANV, ROWS, COLS)).astype(jnp.int32)
    segments = jnp.take_along_axis(segment_start, band_full, axis=1)
    return (band_full * COLS + segments).astype(jnp.int32)


def vector_factor():
    matrix_count = 4 * D * D + 2 * D * FF
    return jnp.where(jnp.arange(P_SIZE) >= matrix_count, 5.0, 1.0).astype(jnp.float32)


def unit_draw(key):
    return jax.random.truncated_normal(key, -3.0, 3.0, (P_SIZE,), jnp.float32)


def draw_params(key, part):
    layout = [(3 * D * D, D ** (-0.5), 0.0), (D * D, (D // 4) ** (-0.5), 0.0), (D * FF, D ** (-0.5), 0.0), (FF * D, FF ** (-0.5), 0.0), (2 * D, 0.2, 0.0), (D, 0.2, 0.0), (FF, 0.2, 0.0), (D, 0.2, 0.0), (D, 0.1, 1.0), (D, 0.2, 0.0), (D, 0.1, 1.0), (D, 0.2, 0.0)]
    scales = jnp.concatenate([jnp.full((amount,), scale_val, jnp.float32) for amount, scale_val, center in layout])
    centers = jnp.concatenate([jnp.full((amount,), center, jnp.float32) for amount, scale_val, center in layout])
    return unit_draw(jax.random.fold_in(key, 21)) * scales + centers


def draw_first_moment(key, part):
    base_scale = 0.111 * (P_SIZE + TABLE * HEADS) ** (-0.5)
    return unit_draw(jax.random.fold_in(key, 31)) * base_scale * vector_factor()


def draw_second_moment(key, part):
    spread = jnp.exp(jax.random.uniform(jax.random.fold_in(key, 41), (P_SIZE,), jnp.float32, math.log(0.5), math.log(8.0)))
    factor_sq = vector_factor() * vector_factor()
    return spread * (0.001 / (P_SIZE + TABLE * HEADS)) * factor_sq


def steps_of(rng, shape, cuts, low, high):
    level = 1.0
    for position, blocks in cuts:
        heights = jax.random.uniform(jax.random.fold_in(jax.random.fold_in(rng, 6), position), (blocks,), jnp.float32, low / len(cuts), high / len(cuts))
        level = level * jnp.repeat(jnp.exp(heights), shape[position] // blocks).reshape((-1,) + (1,) * (len(shape) - 1 - position))
    return level


def bell_draw(stream_key, dims, deviation, limit, cuts=(), kind=jnp.bfloat16):
    level = steps_of(stream_key, dims, cuts, -0.22, 0.18) if cuts else 1.0
    entries = jax.random.normal(stream_key, dims, jnp.float32) * deviation * level
    return jnp.minimum(jnp.maximum(entries, -limit), limit).astype(kind)


def setup_inputs(seed: int = 0) -> dict:
    keys = jax.random.split(jax.random.key(seed), 10)
    return {
        "tokens": bell_draw(keys[0], (NCANV, ROWS, COLS, D), 1.0, 6.0, ((0, 32),)),
        "crop_ids": draw_crop_ids(jax.random.fold_in(keys[9], 71), 0),
        "params": draw_params(jax.random.fold_in(keys[9], 71), 0),
        "first_moment": draw_first_moment(jax.random.fold_in(keys[9], 71), 0),
        "second_moment": draw_second_moment(jax.random.fold_in(keys[9], 71), 0),
        "bias_table": bell_draw(keys[5], (TABLE, HEADS), 1.0, 4.0, (), jnp.float32),
        "table_first": bell_draw(keys[6], (TABLE, HEADS), (0.555 * (P_SIZE + TABLE * HEADS) ** -0.5), 0.005859375, (), jnp.float32),
        "table_second": jnp.clip(jnp.exp(jax.random.uniform(keys[7], (TABLE, HEADS), jnp.float32, math.log(3.3781730190973747e-10), math.log(1.3512692076389499e-09))), 3.3781730190973747e-10, 1.3512692076389499e-09),
        "cotangent": bell_draw(keys[8], (NCANV, ROWS, COLS, D), 1.0, 6.0, ((0, 32),)),
    }


@jax.custom_vjp
def low(v):
    return lax.optimization_barrier(v.astype(jnp.bfloat16)).astype(jnp.float32)

@jax.custom_vjp
def low_back(v):
    return v

def low_keep(v):
    return (low(v), None)

def low_pass(kept, grad):
    return (grad,)

def back_keep(v):
    return (v, None)

def back_low(kept, grad):
    return (low(grad),)
low.defvjp(low_keep, low_pass)
low_back.defvjp(back_keep, back_low)
LEARN_RATE = 0.1
BETA_ONE = 0.9
BETA_TWO = 0.999
ADAM_EPS = 1e-08
WEIGHT_DECAY = 0.05
MAX_NORM = 1.0
NORM_EPS = 1e-05
HIGHEST = lax.Precision.HIGHEST

def unpack(flat):
    layout = ((D, 3 * D), (D, D), (D, FF), (FF, D), (D,), (D,), (D,), (FF,), (D,), (D,), (D,), (D,), (D,))
    pieces = []
    offset = 0
    for dims_of in layout:
        amount = math.prod(dims_of)
        pieces.append(flat[offset:offset + amount].reshape(dims_of))
        offset += amount
    return pieces

def split_windows(field):
    canvases, band_rows, columns, channels = field.shape
    field = field.reshape(canvases, band_rows // WIN, WIN, columns // WIN, WIN, channels)
    return field.transpose(0, 1, 3, 2, 4, 5).reshape(-1, WIN * WIN, channels)

def join_windows(blocks, canvases, band_rows, columns):
    channels = blocks.shape[-1]
    field = blocks.reshape(canvases, band_rows // WIN, columns // WIN, WIN, WIN, channels)
    return field.transpose(0, 1, 3, 2, 4, 5).reshape(canvases, band_rows, columns, channels)

def relative_onehot():
    win_cells = jnp.arange(WIN * WIN)
    cell_rows = win_cells // WIN
    cell_cols = win_cells % WIN
    index = (cell_rows[:, None] - cell_rows[None, :] + WIN - 1) * (2 * WIN - 1) + cell_cols[:, None] - cell_cols[None, :] + WIN - 1
    return (index[:, :, None] == jnp.arange(TABLE)[None, None, :]).astype(jnp.float32)

def layer_norm(values, gain, offset_vec):
    center = values - lax.optimization_barrier(jnp.mean(values, axis=-1, keepdims=True))
    inverse = lax.rsqrt(lax.optimization_barrier(jnp.mean(center * center, axis=-1, keepdims=True)) + NORM_EPS)
    return center * inverse * gain + offset_vec

def window_labels(crop_map):
    rolled = jnp.roll(crop_map, (-SHIFT, -SHIFT), (0, 1))
    row_flag = (jnp.arange(ROWS) >= ROWS - SHIFT).astype(jnp.int32)
    col_flag = (jnp.arange(COLS) >= COLS - SHIFT).astype(jnp.int32)
    return rolled * 4 + 2 * row_flag[:, None] + col_flag[None, :]

def canvas_forward(inputs, crop_map, weights, rel_table):
    w_qkv, w_out, w_up, w_down, b_query, b_value, b_out, b_up, b_down, gain_one, bias_one, gain_two, bias_two = unpack(low(weights))
    normed = low_back(low(layer_norm(inputs, gain_one, bias_one)))
    rolled = jnp.roll(normed, (-SHIFT, -SHIFT), (0, 1))
    blocks = split_windows(rolled[None])
    windows = blocks.shape[0]
    project = jnp.einsum('wid,de->wie', blocks, w_qkv, precision=HIGHEST)
    queries = low_back(low(project[:, :, :D] + b_query)).reshape(windows, WIN * WIN, HEADS, HDIM)
    keys_all = low_back(low(project[:, :, D:2 * D])).reshape(windows, WIN * WIN, HEADS, HDIM)
    values_all = low_back(low(project[:, :, 2 * D:] + b_value)).reshape(windows, WIN * WIN, HEADS, HDIM)
    rel_bias = jnp.einsum('ijt,th->hij', relative_onehot(), rel_table, precision=HIGHEST)
    labels = split_windows(window_labels(crop_map)[None, :, :, None])[:, :, 0]
    allowed = labels[:, :, None] == labels[:, None, :]
    raw_scores = jnp.einsum('wihd,wjhd->whij', queries, keys_all, precision=HIGHEST)
    scores = low_back(raw_scores * HDIM ** (-0.5) + rel_bias[None])
    scores = jnp.where(allowed[:, None], scores, -1e+30)
    row_max = lax.optimization_barrier(jnp.max(scores, axis=-1, keepdims=True))
    exponent = jnp.exp(scores - row_max)
    probabilities = low(exponent / lax.optimization_barrier(jnp.sum(exponent, axis=-1, keepdims=True)))
    mixed_out = jnp.einsum('whij,wjhd->wihd', probabilities, values_all, precision=HIGHEST).reshape(windows, WIN * WIN, D)
    mixed_out = low_back(low(mixed_out))
    mixed_field = jnp.roll(join_windows(mixed_out, 1, ROWS, COLS)[0], (SHIFT, SHIFT), (0, 1))
    attended = low_back(jnp.dot(mixed_field, w_out, precision=HIGHEST) + b_out)
    hidden = inputs + attended
    normed_two = low(layer_norm(hidden, gain_two, bias_two))
    up_proj = low_back(jnp.dot(normed_two, w_up, precision=HIGHEST) + b_up)
    activated = low(jax.nn.gelu(up_proj, approximate=False))
    return hidden + jnp.dot(activated, w_down, precision=HIGHEST) + b_down

def adamw(weights, gradient, first_old, second_old):
    first_new = BETA_ONE * first_old + (1.0 - BETA_ONE) * gradient
    second_new = BETA_TWO * second_old + (1.0 - BETA_TWO) * gradient * gradient
    first_hat = first_new / (1.0 - BETA_ONE ** STEP)
    second_hat = second_new / (1.0 - BETA_TWO ** STEP)
    updated = weights - LEARN_RATE * (first_hat / (jnp.sqrt(second_hat) + ADAM_EPS) + WEIGHT_DECAY * weights)
    return (updated, first_new, second_new)

def reference(tokens, crop_ids, params, first_moment, second_moment, bias_table, table_first, table_second, cotangent):
    canvas_step = jax.checkpoint(canvas_forward)

    def whole(inputs, weights, rel_table):
        return lax.map(lambda paired: canvas_step(paired[0], paired[1], weights, rel_table), (inputs, crop_ids))
    outputs, pullback = jax.vjp(whole, tokens.astype(jnp.float32), params, bias_table)
    grad_tokens, grad_params, grad_table = pullback(cotangent.astype(jnp.float32))
    grad_norm = jnp.sqrt(jnp.sum(grad_params * grad_params) + jnp.sum(grad_table * grad_table))
    factor = jnp.minimum(1.0, MAX_NORM / (grad_norm + 1e-06))
    new_params, new_first, new_second = adamw(params, grad_params * factor, first_moment, second_moment)
    new_table, new_table_first, new_table_second = adamw(bias_table, grad_table * factor, table_first, table_second)
    return (outputs.astype(jnp.bfloat16), grad_tokens, grad_params, grad_table, grad_norm, new_params, new_first, new_second, new_table, new_table_first, new_table_second)
```

```python
from functools import partial
import math

import jax
import jax.numpy as jnp
import numpy as np
from jax import lax
from jax.experimental import pallas as pl
from jax.experimental.pallas import tpu as pltpu
from jax.sharding import PartitionSpec as P

D = 384
HEADS = 12
HDIM = 32
FF = 1536
WIN = 7
CELLS = WIN * WIN
SHIFT = 3
STEP = 10
TABLE = 169
ROWS = 28
BANDS = ROWS // WIN
TOK = ROWS * ROWS
BAND = WIN * ROWS
STRIDE = 8
PAIR = 2
GROUPS = 3
KEYS = 56
LANES = 128
NORM_EPS = 1e-05
SCALE = HDIM**-0.5
BF = jnp.bfloat16
F32 = jnp.float32
NN = (((1,), (0,)), ((), ()))
NT = (((1,), (1,)), ((), ()))
TN = (((0,), (0,)), ((), ()))
CHUNK = 112

V_BQ, V_BV, V_BO, V_BUP, V_BDN, V_G1, V_B1, V_G2, V_B2 = range(9)


def dg(a, b, dims):
    return lax.dot_general(a, b, dims, preferred_element_type=F32)


def lanes_iota(rows):
    return lax.broadcasted_iota(jnp.int32, (rows, LANES), 1)


def split_keys(block):
    odd = (lanes_iota(KEYS) // HDIM) % 2 == 1
    return jnp.concatenate([jnp.where(odd, 0.0, block), jnp.where(odd, block, 0.0)], axis=0).astype(BF)


def join_keys(both):
    odd = (lanes_iota(KEYS) // HDIM) % 2 == 1
    return jnp.where(odd, both[KEYS:], both[:KEYS])


def split_queries(block):
    high = lanes_iota(KEYS) >= 64
    live = lax.broadcasted_iota(jnp.int32, (KEYS, LANES), 0) < CELLS
    zero = jnp.zeros((8, LANES), F32)
    low_part = jnp.where(jnp.logical_and(live, jnp.logical_not(high)), block, 0.0)
    high_part = jnp.where(jnp.logical_and(live, high), block, 0.0)
    return jnp.concatenate([low_part, zero, high_part, zero], axis=0).astype(BF)


def join_queries(both):
    high = lanes_iota(KEYS) >= 64
    return jnp.where(high, both[64 : 64 + KEYS], both[:KEYS])


def block_kernel(
    canv, tok_hbm, cot_hbm, lab_ref, bias_ref, wqkv_ref, wout_ref, wup_ref, wdn_ref, vec_ref,
    out_hbm, gtok_hbm, gqkv_ref, gout_ref, gup_ref, gdn_ref, gvec_ref, gbias_ref,
    tokb, cotb, outb, gtb, sems,
    cotw, nm, qkv, prob, mix, mixb, hid, nt, n2, inv2, act, gup_act, ght, gab, dqkv, dqb, tmp, tmp3,
):
    step = pl.program_id(0)
    steps = pl.num_programs(0)
    slot = lax.rem(step, 2)
    wrows = CELLS * canv
    rows_all = PAIR * wrows

    def copies(kind, hbm, buf, at, where):
        made = []
        for u in range(PAIR):
            w = at * PAIR + u
            wr, wc = w // BANDS, lax.rem(w, BANDS)
            for ra, rn in ((0, 4), (4, 3)):
                r0 = lax.rem(WIN * wr + SHIFT + ra, ROWS)
                for ca, cn in ((0, 4), (4, 3)):
                    c0 = lax.rem(WIN * wc + SHIFT + ca, ROWS)
                    far = hbm.at[pl.ds(r0, rn), pl.ds(c0, cn)]
                    near = buf.at[where, u, pl.ds(ra, rn), pl.ds(ca, cn)]
                    sem = sems.at[kind, where, len(made)]
                    made.append(
                        pltpu.make_async_copy(far, near, sem) if kind < 2 else pltpu.make_async_copy(near, far, sem)
                    )
        return made

    def begin(*what):
        for copy in copies(*what):
            copy.start()

    def finish(*what):
        for copy in copies(*what):
            copy.wait()

    @pl.when(step == 0)
    def _():
        begin(0, tok_hbm, tokb, step, slot)
        begin(1, cot_hbm, cotb, step, slot)
        for ref in (gqkv_ref, gout_ref, gup_ref, gdn_ref, gvec_ref, gbias_ref):
            ref[...] = jnp.zeros_like(ref)
        for ref in (qkv, tmp3):
            ref[:, rows_all:] = jnp.zeros((ref.shape[0], ref.shape[1] - rows_all, LANES), F32)

    @pl.when(step + 1 < steps)
    def _():
        begin(0, tok_hbm, tokb, step + 1, 1 - slot)
        begin(1, cot_hbm, cotb, step + 1, 1 - slot)

    finish(0, tok_hbm, tokb, step, slot)
    finish(1, cot_hbm, cotb, step, slot)

    @pl.when(step >= 2)
    def _():
        finish(2, out_hbm, outb, step - 2, slot)
        finish(3, gtok_hbm, gtb, step - 2, slot)

    def vec(row, width=D):
        return vec_ref[row : row + 1, :width]

    def add_vec(row, value, start=0):
        width = value.shape[1]
        gvec_ref[row : row + 1, start : start + width] += value

    def col_sum(value):
        return jnp.sum(value, axis=0, keepdims=True)

    def cell_rows(body):
        def one(i, carry):
            u = i // WIN
            body(pl.ds(pl.multiple_of(i * WIN * canv, 8), WIN * canv), u, lax.rem(i, WIN))
            return carry

        lax.fori_loop(0, PAIR * WIN, one, 0)

    def chunks(body):
        def one(i, carry):
            body(pl.ds(pl.multiple_of(i * CHUNK, CHUNK), CHUNK))
            return carry

        lax.fori_loop(0, rows_all // CHUNK, one, 0)

    def stats(x):
        center = x - jnp.mean(x, axis=-1, keepdims=True)
        inv = lax.rsqrt(jnp.mean(center * center, axis=-1, keepdims=True) + NORM_EPS)
        return center * inv, inv

    def load_cells(buf, u, a):
        return buf[slot, u, a].astype(F32).reshape(WIN * canv, D)

    CW = 2 * WIN * canv

    def double_rows(body):
        def one(i, carry):
            body(pl.ds(pl.multiple_of(i * CW, 16), CW), [((2 * i + k) // WIN, lax.rem(2 * i + k, WIN)) for k in range(2)])
            return carry

        lax.fori_loop(0, WIN, one, 0)

    def load_two(buf, places):
        return jnp.concatenate([load_cells(buf, u, a) for u, a in places], axis=0)

    def norm_one(rows, places):
        x = load_two(tokb, places)
        n1, _ = stats(x)
        nm[rows] = (n1 * vec(V_G1) + vec(V_B1)).astype(BF)
        cotw[rows] = load_two(cotb, places).astype(BF)
        hid[rows] = x

    double_rows(norm_one)

    for j in range(3):
        cols = slice(j * D, (j + 1) * D)
        part = dg(nm[...], wqkv_ref[:, cols], NN)
        if j == 0:
            part = part + vec(V_BQ)
        if j == 2:
            part = part + vec(V_BV)
        for g in range(GROUPS):
            qkv[j * GROUPS + g, :rows_all] = part[:, g * LANES : (g + 1) * LANES]

    UNROLL = 2

    def view(ref, which, u):
        return ref.at[which, pl.ds(pl.multiple_of(u * wrows, 8), KEYS * canv)]

    def take(ref, which, u, c):
        return view(ref, which, u)[pl.ds(c, KEYS, stride=canv)]

    def put(ref, which, u, c, value):
        view(ref, which, u)[pl.ds(c, CELLS, stride=canv)] = value[:CELLS]

    def attend_all(u, carry):
        for v in range(0, canv, UNROLL):
            attend(u, range(v, v + UNROLL))
        return carry

    def attend(u, cs):
        items = [(c, g) for c in cs for g in range(GROUPS)]
        masks = {}
        for c in cs:
            row = lab_ref[u, c : c + 1, :]
            col = jnp.transpose(jnp.broadcast_to(row, (LANES, LANES)))[:KEYS]
            masks[c] = (col == row)[None]
        raw = []
        for c, g in items:
            q2 = split_queries(take(qkv, g, u, c))
            k2 = split_keys(take(qkv, GROUPS + g, u, c))
            raw.append(dg(k2, q2, NT))
        probs = []
        for (c, g), s in zip(items, raw):
            s = (s * SCALE + bias_ref[g]).reshape(2, KEYS, LANES)
            s = jnp.where(masks[c], s, -1e30)
            e = jnp.exp(s - jnp.max(s, axis=1, keepdims=True))
            p = e * (1.0 / jnp.sum(e, axis=1, keepdims=True))
            p = p.reshape(2 * KEYS, LANES)
            prob[u, c * GROUPS + g] = p
            probs.append(p.astype(BF))
        outs = []
        for (c, g), p in zip(items, probs):
            v2 = split_keys(take(qkv, 2 * GROUPS + g, u, c))
            outs.append(join_queries(dg(p, v2, TN)))
        for (c, g), o in zip(items, outs):
            put(mix, g, u, c, o)

    lax.fori_loop(0, PAIR, attend_all, 0)

    for g in range(GROUPS):
        mixb[:, g * LANES : (g + 1) * LANES] = mix[g, :rows_all].astype(BF)
    hid[...] += dg(mixb[...], wout_ref[...], NN) + vec(V_BO)

    def norm_two(rows):
        n, inv = stats(hid[rows])
        n2[rows] = n
        inv2[rows] = inv
        nt[rows] = (n * vec(V_G2) + vec(V_B2)).astype(BF)

    chunks(norm_two)

    FC = 512
    for f in range(FF // FC):
        cols = slice(f * FC, (f + 1) * FC)
        up = dg(nt[...], wup_ref[:, cols], NN) + vec_ref[V_BUP : V_BUP + 1, cols]
        dact = dg(cotw[...], wdn_ref[cols, :], NT)
        cdf = 0.5 + 0.5 * lax.erf(up * (0.5**0.5))
        act[:, cols] = (up * cdf).astype(BF)
        slope = cdf + up * (jnp.exp(-0.5 * up * up) * (1.0 / math.sqrt(2.0 * math.pi)))
        gu = (dact * slope).astype(BF)
        gup_act[:, cols] = gu
        add_vec(V_BUP, col_sum(gu.astype(F32)), f * FC)
    for f in range(FF // FC):
        cols = slice(f * FC, (f + 1) * FC)
        gup_ref[:, cols] += dg(nt[...], gup_act[:, cols], TN)
        gdn_ref[:, cols] += dg(cotw[...], act[:, cols], TN)
    tmp[...] = hid[...] + dg(act[...], wdn_ref[...], NN) + vec(V_BDN)

    def store_out(rows, u, a):
        outb[slot, u, a] = tmp[rows].reshape(WIN, canv, D).astype(BF)

    cell_rows(store_out)
    begin(2, out_hbm, outb, step, slot)
    tmp[...] = dg(gup_act[...], wup_ref[...], NT)

    def back_two(rows):
        gn = tmp[rows]
        n = n2[rows]
        c = cotw[rows].astype(F32)
        add_vec(V_G2, col_sum(gn * n))
        add_vec(V_B2, col_sum(gn))
        add_vec(V_BDN, col_sum(c))
        e = gn * vec(V_G2)
        g = c + inv2[rows] * (
            e - jnp.mean(e, axis=-1, keepdims=True) - n * jnp.mean(e * n, axis=-1, keepdims=True)
        )
        ght[rows] = g
        low = g.astype(BF)
        gab[rows] = low
        add_vec(V_BO, col_sum(low.astype(F32)))

    chunks(back_two)

    gout_ref[...] += dg(mixb[...], gab[...], TN)
    part = dg(gab[...], wout_ref[...], NT)
    for g in range(GROUPS):
        tmp3[g, :rows_all] = part[:, g * LANES : (g + 1) * LANES]

    def back_all(u, carry):
        for v in range(0, canv, UNROLL):
            attend_back(u, range(v, v + UNROLL))
        return carry

    def attend_back(u, cs):
        items = [(c, g) for c in cs for g in range(GROUPS)]
        o2s, raws = [], []
        for c, g in items:
            v2 = split_keys(take(qkv, 2 * GROUPS + g, u, c))
            o2 = split_queries(take(tmp3, g, u, c))
            raws.append(dg(v2, o2, NT))
            o2s.append(o2)
        dss, gvs = [], []
        for (c, g), dp, o2 in zip(items, raws, o2s):
            p = prob[u, c * GROUPS + g]
            gvs.append(join_keys(dg(p.astype(BF), o2, NN)))
            p3 = p.reshape(2, KEYS, LANES)
            dp3 = dp.reshape(2, KEYS, LANES)
            ds = p3 * (dp3 - jnp.sum(p3 * dp3, axis=1, keepdims=True))
            low = ds.reshape(2 * KEYS, LANES).astype(BF)
            gbias_ref[g] += low.astype(F32)
            dss.append(low)
        gqs, gks = [], []
        for (c, g), ds in zip(items, dss):
            q2 = split_queries(take(qkv, g, u, c))
            k2 = split_keys(take(qkv, GROUPS + g, u, c))
            gks.append(join_keys(dg(ds, q2, NN)) * SCALE)
            gqs.append(join_queries(dg(ds, k2, TN)) * SCALE)
        for (c, g), gq, gk, gv in zip(items, gqs, gks, gvs):
            put(dqkv, g, u, c, gq)
            put(dqkv, GROUPS + g, u, c, gk)
            put(dqkv, 2 * GROUPS + g, u, c, gv)

    lax.fori_loop(0, PAIR, back_all, 0)

    def round_back(rows):
        for j in range(3 * GROUPS):
            low = dqkv[j, rows].astype(BF)
            dqb[rows, j * LANES : (j + 1) * LANES] = low
            if j < GROUPS:
                add_vec(V_BQ, col_sum(low.astype(F32)), j * LANES)
            elif j >= 2 * GROUPS:
                add_vec(V_BV, col_sum(low.astype(F32)), (j - 2 * GROUPS) * LANES)

    chunks(round_back)
    gqkv_ref[...] += dg(nm[...], dqb[...], TN)
    tmp[...] = dg(dqb[...], wqkv_ref[...], NT)

    def back_one(rows, u, a):
        gn = tmp[rows].astype(BF).astype(F32)
        n, inv = stats(load_cells(tokb, u, a))
        add_vec(V_G1, col_sum(gn * n))
        add_vec(V_B1, col_sum(gn))
        e = gn * vec(V_G1)
        g = ght[rows] + inv * (
            e - jnp.mean(e, axis=-1, keepdims=True) - n * jnp.mean(e * n, axis=-1, keepdims=True)
        )
        gtb[slot, u, a] = g.reshape(WIN, canv, D)

    cell_rows(back_one)
    begin(3, gtok_hbm, gtb, step, slot)

    @pl.when(step + 1 == steps)
    def _():
        for back in (1, 0):
            finish(2, out_hbm, outb, step - back, slot if back == 0 else 1 - slot)
            finish(3, gtok_hbm, gtb, step - back, slot if back == 0 else 1 - slot)


def block_call(tokens, cot, labels, bias, wqkv, wout, wup, wdn, vecs):
    canv = tokens.shape[2]
    rows = PAIR * CELLS * canv
    tall = (PAIR - 1) * CELLS * canv + KEYS * canv
    hbm = pl.BlockSpec(memory_space=pl.ANY)

    def whole(*shape):
        return pl.BlockSpec(shape, lambda i: (0,) * len(shape), pipeline_mode=pl.Buffered(1))

    sums = [
        ((D, 3 * D), F32), ((D, D), F32), ((D, FF), F32), ((D, FF), F32), ((16, FF), F32), ((GROUPS, 2 * KEYS, LANES), F32),
    ]
    cells = (2, PAIR, WIN, WIN, canv, D)
    return pl.pallas_call(
        partial(block_kernel, canv),
        grid=(BANDS * BANDS // PAIR,),
        out_shape=[
            jax.ShapeDtypeStruct(tokens.shape, BF),
            jax.ShapeDtypeStruct(tokens.shape, F32),
            *[jax.ShapeDtypeStruct(s, d) for s, d in sums],
        ],
        in_specs=[
            hbm, hbm,
            pl.BlockSpec((PAIR, canv, LANES), lambda i: (i, 0, 0)),
            whole(GROUPS, 2 * KEYS, LANES),
            whole(D, 3 * D), whole(D, D), whole(D, FF), whole(FF, D), whole(16, FF),
        ],
        out_specs=[hbm, hbm, *[whole(*s) for s, _ in sums]],
        scratch_shapes=[
            pltpu.VMEM(cells, BF),
            pltpu.VMEM(cells, BF),
            pltpu.VMEM(cells, BF),
            pltpu.VMEM(cells, F32),
            pltpu.SemaphoreType.DMA((4, 2, 4 * PAIR)),
            pltpu.VMEM((rows, D), BF),
            pltpu.VMEM((rows, D), BF),
            pltpu.VMEM((3 * GROUPS, tall, LANES), F32),
            pltpu.VMEM((PAIR, canv * GROUPS, 2 * KEYS, LANES), F32),
            pltpu.VMEM((GROUPS, tall, LANES), F32),
            pltpu.VMEM((rows, D), BF),
            pltpu.VMEM((rows, D), F32),
            pltpu.VMEM((rows, D), BF),
            pltpu.VMEM((rows, D), F32),
            pltpu.VMEM((rows, 1), F32),
            pltpu.VMEM((rows, FF), BF),
            pltpu.VMEM((rows, FF), BF),
            pltpu.VMEM((rows, D), F32),
            pltpu.VMEM((rows, D), BF),
            pltpu.VMEM((3 * GROUPS, tall, LANES), F32),
            pltpu.VMEM((rows, 3 * D), BF),
            pltpu.VMEM((rows, D), F32),
            pltpu.VMEM((GROUPS, tall, LANES), F32),
        ],
        compiler_params=pltpu.CompilerParams(vmem_limit_bytes=63 << 20),
        name="block",
    )(tokens, cot, labels, bias, wqkv, wout, wup, wdn, vecs)


def unpack(flat):
    layout = ((D, 3 * D), (D, D), (D, FF), (FF, D), (D,), (D,), (D,), (FF,), (D,), (D,), (D,), (D,), (D,))
    pieces = []
    offset = 0
    for dims_of in layout:
        amount = math.prod(dims_of)
        pieces.append(flat[offset : offset + amount].reshape(dims_of))
        offset += amount
    return pieces


def split_windows(field):
    canvases, band_rows, columns, channels = field.shape
    field = field.reshape(canvases, band_rows // WIN, WIN, columns // WIN, WIN, channels)
    return field.transpose(0, 1, 3, 2, 4, 5).reshape(-1, WIN * WIN, channels)


def window_labels(crop_ids):
    canvases, height, columns = crop_ids.shape
    crop_roll = jnp.roll(crop_ids, (-SHIFT, -SHIFT), (1, 2))
    row_flag = (jnp.arange(height, dtype=jnp.int32) >= height - SHIFT).astype(jnp.int32)
    col_flag = (jnp.arange(columns, dtype=jnp.int32) >= columns - SHIFT).astype(jnp.int32)
    labels = crop_roll * 4 + 2 * row_flag[None, :, None] + col_flag[None, None, :]
    labels = split_windows(labels[..., None])[:, :, 0].reshape(canvases, -1, CELLS)
    labels = jnp.pad(labels, ((0, 0), (0, 0), (0, 64 - CELLS)), constant_values=-1)
    return jnp.concatenate([labels, labels], axis=-1).astype(F32).transpose(1, 0, 2)


def offset_onehot():
    cells = np.arange(CELLS)
    r, c = cells // WIN, cells % WIN
    index = (r[None, :] - r[:, None] + WIN - 1) * (2 * WIN - 1) + c[None, :] - c[:, None] + WIN - 1
    hot = np.zeros((KEYS, 64, TABLE), np.float32)
    hot[:CELLS, :CELLS] = index[:, :, None] == np.arange(TABLE)
    return hot


def pair_bias(table):
    hot = jnp.asarray(offset_onehot(), BF).astype(F32)
    full = jnp.einsum("jit,th->hji", hot, table, precision=lax.Precision.HIGHEST)
    full = full.reshape(GROUPS, 2, 2, KEYS, 64).transpose(0, 2, 3, 1, 4)
    return full.reshape(GROUPS, 2 * KEYS, LANES)


def table_sum(gbias):
    hot = jnp.asarray(offset_onehot(), BF).astype(F32)
    full = gbias.reshape(GROUPS, 2, KEYS, 2, 64).transpose(0, 3, 1, 2, 4).reshape(HEADS, KEYS, 64)
    return jnp.einsum("jit,hji->th", hot, full, precision=lax.Precision.HIGHEST)


def local_block(tokens, crop_ids, flat_low, bias_table, cotangent):
    p = unpack(flat_low)
    vecs = jnp.concatenate([jnp.pad(v, (0, FF - v.shape[0]))[None] for v in p[4:]], axis=0)
    vecs = jnp.pad(vecs, ((0, 7), (0, 0))).astype(F32)
    out = block_call(tokens.transpose(1, 2, 0, 3), cotangent.transpose(1, 2, 0, 3), window_labels(crop_ids), pair_bias(bias_table), p[0], p[1], p[2], p[3], vecs)
    out_tokens, grad_tokens, gqkv, gout, gup, gdn, gvec, gbias = out
    widths = [D, D, D, FF, D, D, D, D, D]
    flat = jnp.concatenate(
        [gqkv.ravel(), gout.ravel(), gup.ravel(), gdn.T.ravel()] + [gvec[i, :w] for i, w in enumerate(widths)]
    )
    return out_tokens.transpose(2, 0, 1, 3), grad_tokens.transpose(2, 0, 1, 3), flat, table_sum(gbias)


LEARN_RATE = 0.1
BETA_ONE = 0.9
BETA_TWO = 0.999
ADAM_EPS = 1e-08
WEIGHT_DECAY = 0.05
MAX_NORM = 1.0


def adamw(weights, gradient, first_old, second_old):
    first_new = BETA_ONE * first_old + (1.0 - BETA_ONE) * gradient
    second_new = BETA_TWO * second_old + (1.0 - BETA_TWO) * gradient * gradient
    first_hat = first_new / (1.0 - BETA_ONE**STEP)
    second_hat = second_new / (1.0 - BETA_TWO**STEP)
    updated = weights - LEARN_RATE * (first_hat / (jnp.sqrt(second_hat) + ADAM_EPS) + WEIGHT_DECAY * weights)
    return (updated, first_new, second_new)


def local(tokens, crop_ids, params, first_moment, second_moment, bias_table, table_first, table_second, cotangent):
    axes = ("dp", "shard")
    flat_low = lax.all_gather(params.astype(BF), axes, axis=0, tiled=True)
    out_tokens, grad_tokens, local_grad, g_table = local_block(tokens, crop_ids, flat_low, bias_table, cotangent)
    grad_shard = lax.psum_scatter(local_grad, axes, scatter_dimension=0, tiled=True)
    table_grad, square_sum = lax.psum((g_table, jnp.sum(grad_shard * grad_shard)), axes)
    grad_norm = jnp.sqrt(square_sum + jnp.sum(table_grad * table_grad))
    factor = jnp.minimum(1.0, MAX_NORM / (grad_norm + 1e-06))
    new_params, new_first, new_second = adamw(params, grad_shard * factor, first_moment, second_moment)
    new_table, new_table_first, new_table_second = adamw(bias_table, table_grad * factor, table_first, table_second)
    return (
        out_tokens, grad_tokens, grad_shard, table_grad, grad_norm, new_params, new_first, new_second,
        new_table, new_table_first, new_table_second,
    )


def solution(mesh):
    both = P(("dp", "shard"))
    return jax.shard_map(
        local,
        mesh=mesh,
        in_specs=(both, both, both, both, both, P(), P(), P(), both),
        out_specs=(both, both, both, P(), P(), both, both, both, P(), P(), P()),
        check_vma=False,
    )
```

```python
from functools import partial
import math

import jax
import jax.numpy as jnp
import numpy as np
from jax import lax
from jax.experimental import pallas as pl
from jax.experimental.pallas import tpu as pltpu
from jax.sharding import PartitionSpec as P

D = 384
HEADS = 12
HDIM = 32
FF = 1536
WIN = 7
CELLS = WIN * WIN
SHIFT = 3
STEP = 10
TABLE = 169
ROWS = 28
BANDS = ROWS // WIN
TOK = ROWS * ROWS
BAND = WIN * ROWS
STRIDE = 8
PAIR = 2
GROUPS = 3
KEYS = 56
LANES = 128
NORM_EPS = 1e-05
SCALE = HDIM**-0.5
BF = jnp.bfloat16
F32 = jnp.float32
NN = (((1,), (0,)), ((), ()))
NT = (((1,), (1,)), ((), ()))
TN = (((0,), (0,)), ((), ()))
CHUNK = 112

V_BQ, V_BV, V_BO, V_BUP, V_BDN, V_G1, V_B1, V_G2, V_B2 = range(9)


def dg(a, b, dims):
    return lax.dot_general(a, b, dims, preferred_element_type=F32)


def lanes_iota(rows):
    return lax.broadcasted_iota(jnp.int32, (rows, LANES), 1)


def split_keys(block):
    odd = (lanes_iota(KEYS) // HDIM) % 2 == 1
    return jnp.concatenate([jnp.where(odd, 0.0, block), jnp.where(odd, block, 0.0)], axis=0).astype(BF)


def join_keys(both):
    odd = (lanes_iota(KEYS) // HDIM) % 2 == 1
    return jnp.where(odd, both[KEYS:], both[:KEYS])


def split_queries(block):
    high = lanes_iota(KEYS) >= 64
    live = lax.broadcasted_iota(jnp.int32, (KEYS, LANES), 0) < CELLS
    zero = jnp.zeros((8, LANES), F32)
    low_part = jnp.where(jnp.logical_and(live, jnp.logical_not(high)), block, 0.0)
    high_part = jnp.where(jnp.logical_and(live, high), block, 0.0)
    return jnp.concatenate([low_part, zero, high_part, zero], axis=0).astype(BF)


def join_queries(both):
    high = lanes_iota(KEYS) >= 64
    return jnp.where(high, both[64 : 64 + KEYS], both[:KEYS])


def block_kernel(
    canv, starts, tok_hbm, cot_hbm, lab_ref, bias_ref, parts_hbm,
    out_hbm, gtok_hbm, send_ref, gbias_ref,
    flat, wqkv_ref, wout_ref, wup_ref, wdn_ref, vec_ref, gqkv_ref, gout_ref, gup_ref, gdn_ref, gvec_ref, parts_sem,
    tokb, cotb, outb, gtb, sems,
    cotw, nm, qkv, prob, mix, mixb, hid, nt, n2, inv2, act, gup_act, ght, gab, dqkv, dqb, tmp, tmp3,
):
    step = pl.program_id(0)
    steps = pl.num_programs(0)
    slot = lax.rem(step, 2)
    wrows = CELLS * canv
    rows_all = PAIR * wrows

    def copies(kind, hbm, buf, at, where):
        made = []
        for u in range(PAIR):
            w = at * PAIR + u
            wr, wc = w // BANDS, lax.rem(w, BANDS)
            for ra, rn in ((0, 4), (4, 3)):
                r0 = lax.rem(WIN * wr + SHIFT + ra, ROWS)
                for ca, cn in ((0, 4), (4, 3)):
                    c0 = lax.rem(WIN * wc + SHIFT + ca, ROWS)
                    far = hbm.at[pl.ds(r0, rn), pl.ds(c0, cn)]
                    near = buf.at[where, u, pl.ds(ra, rn), pl.ds(ca, cn)]
                    sem = sems.at[kind, where, len(made)]
                    made.append(
                        pltpu.make_async_copy(far, near, sem) if kind < 2 else pltpu.make_async_copy(near, far, sem)
                    )
        return made

    def begin(*what):
        for copy in copies(*what):
            copy.start()

    def finish(*what):
        for copy in copies(*what):
            copy.wait()

    @pl.when(step == 0)
    def _():
        gathered = pltpu.make_async_copy(parts_hbm, send_ref, parts_sem)
        gathered.start()
        begin(0, tok_hbm, tokb, step, slot)
        begin(1, cot_hbm, cotb, step, slot)
        for ref in (gqkv_ref, gout_ref, gup_ref, gdn_ref, gvec_ref, gbias_ref):
            ref[...] = jnp.zeros_like(ref)
        for ref in (qkv, tmp3):
            ref[:, rows_all:] = jnp.zeros((ref.shape[0], ref.shape[1] - rows_all, LANES), F32)
        gathered.wait()
        flat[:8] = jnp.zeros((8, LANES), F32)
        for k, start in enumerate(starts):
            part = send_ref[k].astype(F32)
            first = part[:8] + jnp.where(lax.broadcasted_iota(jnp.int32, (8, LANES), 0) == 0, flat[start : start + 8], 0.0)
            flat[start : start + 8] = first
            flat[start + 8 : start + part.shape[0]] = part[8:]
        for ref, base in matrices((wqkv_ref, wout_ref, wup_ref, wdn_ref)):
            wide = ref.shape[1] // LANES
            for j in range(wide):
                ref[:, j * LANES : (j + 1) * LANES] = flat[pl.ds(base + j, ref.shape[0], stride=wide)].astype(BF)
        for row, j, at in vector_rows():
            vec_ref[row : row + 1, j * LANES : (j + 1) * LANES] = flat[at : at + 1]

    @pl.when(step + 1 < steps)
    def _():
        begin(0, tok_hbm, tokb, step + 1, 1 - slot)
        begin(1, cot_hbm, cotb, step + 1, 1 - slot)

    finish(0, tok_hbm, tokb, step, slot)
    finish(1, cot_hbm, cotb, step, slot)

    @pl.when(step >= 2)
    def _():
        finish(2, out_hbm, outb, step - 2, slot)
        finish(3, gtok_hbm, gtb, step - 2, slot)

    def vec(row, width=D):
        return vec_ref[row : row + 1, :width]

    def add_vec(row, value, start=0):
        width = value.shape[1]
        gvec_ref[row : row + 1, start : start + width] += value

    def col_sum(value):
        return jnp.sum(value, axis=0, keepdims=True)

    def cell_rows(body):
        def one(i, carry):
            u = i // WIN
            body(pl.ds(pl.multiple_of(i * WIN * canv, 8), WIN * canv), u, lax.rem(i, WIN))
            return carry

        lax.fori_loop(0, PAIR * WIN, one, 0)

    def chunks(body):
        def one(i, carry):
            body(pl.ds(pl.multiple_of(i * CHUNK, CHUNK), CHUNK))
            return carry

        lax.fori_loop(0, rows_all // CHUNK, one, 0)

    def stats(x):
        center = x - jnp.mean(x, axis=-1, keepdims=True)
        inv = lax.rsqrt(jnp.mean(center * center, axis=-1, keepdims=True) + NORM_EPS)
        return center * inv, inv

    def load_cells(buf, u, a):
        return buf[slot, u, a].astype(F32).reshape(WIN * canv, D)

    CW = 2 * WIN * canv

    def double_rows(body):
        def one(i, carry):
            body(pl.ds(pl.multiple_of(i * CW, 16), CW), [((2 * i + k) // WIN, lax.rem(2 * i + k, WIN)) for k in range(2)])
            return carry

        lax.fori_loop(0, WIN, one, 0)

    def load_two(buf, places):
        return jnp.concatenate([load_cells(buf, u, a) for u, a in places], axis=0)

    def norm_one(rows, places):
        x = load_two(tokb, places)
        n1, _ = stats(x)
        nm[rows] = (n1 * vec(V_G1) + vec(V_B1)).astype(BF)
        cotw[rows] = load_two(cotb, places).astype(BF)
        hid[rows] = x

    double_rows(norm_one)

    for j in range(3):
        cols = slice(j * D, (j + 1) * D)
        part = dg(nm[...], wqkv_ref[:, cols], NN)
        if j == 0:
            part = part + vec(V_BQ)
        if j == 2:
            part = part + vec(V_BV)
        for g in range(GROUPS):
            qkv[j * GROUPS + g, :rows_all] = part[:, g * LANES : (g + 1) * LANES]

    UNROLL = 2

    def view(ref, which, u):
        return ref.at[which, pl.ds(pl.multiple_of(u * wrows, 8), KEYS * canv)]

    def take(ref, which, u, c):
        return view(ref, which, u)[pl.ds(c, KEYS, stride=canv)]

    def put(ref, which, u, c, value):
        view(ref, which, u)[pl.ds(c, CELLS, stride=canv)] = value[:CELLS]

    def attend_all(u, carry):
        for v in range(0, canv, UNROLL):
            attend(u, range(v, v + UNROLL))
        return carry

    def attend(u, cs):
        items = [(c, g) for c in cs for g in range(GROUPS)]
        masks = {}
        for c in cs:
            row = lab_ref[u, c : c + 1, :]
            col = jnp.transpose(jnp.broadcast_to(row, (LANES, LANES)))[:KEYS]
            masks[c] = (col == row)[None]
        raw = []
        for c, g in items:
            q2 = split_queries(take(qkv, g, u, c))
            k2 = split_keys(take(qkv, GROUPS + g, u, c))
            raw.append(dg(k2, q2, NT))
        probs = []
        for (c, g), s in zip(items, raw):
            s = (s * SCALE + bias_ref[g]).reshape(2, KEYS, LANES)
            s = jnp.where(masks[c], s, -1e30)
            e = jnp.exp(s - jnp.max(s, axis=1, keepdims=True))
            p = e * (1.0 / jnp.sum(e, axis=1, keepdims=True))
            p = p.reshape(2 * KEYS, LANES)
            prob[u, c * GROUPS + g] = p
            probs.append(p.astype(BF))
        outs = []
        for (c, g), p in zip(items, probs):
            v2 = split_keys(take(qkv, 2 * GROUPS + g, u, c))
            outs.append(join_queries(dg(p, v2, TN)))
        for (c, g), o in zip(items, outs):
            put(mix, g, u, c, o)

    lax.fori_loop(0, PAIR, attend_all, 0)

    for g in range(GROUPS):
        mixb[:, g * LANES : (g + 1) * LANES] = mix[g, :rows_all].astype(BF)
    hid[...] += dg(mixb[...], wout_ref[...], NN) + vec(V_BO)

    def norm_two(rows):
        n, inv = stats(hid[rows])
        n2[rows] = n
        inv2[rows] = inv
        nt[rows] = (n * vec(V_G2) + vec(V_B2)).astype(BF)

    chunks(norm_two)

    FC = 512
    for f in range(FF // FC):
        cols = slice(f * FC, (f + 1) * FC)
        up = dg(nt[...], wup_ref[:, cols], NN) + vec_ref[V_BUP : V_BUP + 1, cols]
        dact = dg(cotw[...], wdn_ref[cols, :], NT)
        cdf = 0.5 + 0.5 * lax.erf(up * (0.5**0.5))
        act[:, cols] = (up * cdf).astype(BF)
        slope = cdf + up * (jnp.exp(-0.5 * up * up) * (1.0 / math.sqrt(2.0 * math.pi)))
        gu = (dact * slope).astype(BF)
        gup_act[:, cols] = gu
        add_vec(V_BUP, col_sum(gu.astype(F32)), f * FC)
    for f in range(FF // FC):
        cols = slice(f * FC, (f + 1) * FC)
        gup_ref[:, cols] += dg(nt[...], gup_act[:, cols], TN)
        gdn_ref[:, cols] += dg(cotw[...], act[:, cols], TN)
    tmp[...] = hid[...] + dg(act[...], wdn_ref[...], NN) + vec(V_BDN)

    def store_out(rows, u, a):
        outb[slot, u, a] = tmp[rows].reshape(WIN, canv, D).astype(BF)

    cell_rows(store_out)
    begin(2, out_hbm, outb, step, slot)
    tmp[...] = dg(gup_act[...], wup_ref[...], NT)

    def back_two(rows):
        gn = tmp[rows]
        n = n2[rows]
        c = cotw[rows].astype(F32)
        add_vec(V_G2, col_sum(gn * n))
        add_vec(V_B2, col_sum(gn))
        add_vec(V_BDN, col_sum(c))
        e = gn * vec(V_G2)
        g = c + inv2[rows] * (
            e - jnp.mean(e, axis=-1, keepdims=True) - n * jnp.mean(e * n, axis=-1, keepdims=True)
        )
        ght[rows] = g
        low = g.astype(BF)
        gab[rows] = low
        add_vec(V_BO, col_sum(low.astype(F32)))

    chunks(back_two)

    gout_ref[...] += dg(mixb[...], gab[...], TN)
    part = dg(gab[...], wout_ref[...], NT)
    for g in range(GROUPS):
        tmp3[g, :rows_all] = part[:, g * LANES : (g + 1) * LANES]

    def back_all(u, carry):
        for v in range(0, canv, UNROLL):
            attend_back(u, range(v, v + UNROLL))
        return carry

    def attend_back(u, cs):
        items = [(c, g) for c in cs for g in range(GROUPS)]
        o2s, raws = [], []
        for c, g in items:
            v2 = split_keys(take(qkv, 2 * GROUPS + g, u, c))
            o2 = split_queries(take(tmp3, g, u, c))
            raws.append(dg(v2, o2, NT))
            o2s.append(o2)
        dss, gvs = [], []
        for (c, g), dp, o2 in zip(items, raws, o2s):
            p = prob[u, c * GROUPS + g]
            gvs.append(join_keys(dg(p.astype(BF), o2, NN)))
            p3 = p.reshape(2, KEYS, LANES)
            dp3 = dp.reshape(2, KEYS, LANES)
            ds = p3 * (dp3 - jnp.sum(p3 * dp3, axis=1, keepdims=True))
            low = ds.reshape(2 * KEYS, LANES).astype(BF)
            gbias_ref[g] += low.astype(F32)
            dss.append(low)
        gqs, gks = [], []
        for (c, g), ds in zip(items, dss):
            q2 = split_queries(take(qkv, g, u, c))
            k2 = split_keys(take(qkv, GROUPS + g, u, c))
            gks.append(join_keys(dg(ds, q2, NN)) * SCALE)
            gqs.append(join_queries(dg(ds, k2, TN)) * SCALE)
        for (c, g), gq, gk, gv in zip(items, gqs, gks, gvs):
            put(dqkv, g, u, c, gq)
            put(dqkv, GROUPS + g, u, c, gk)
            put(dqkv, 2 * GROUPS + g, u, c, gv)

    lax.fori_loop(0, PAIR, back_all, 0)

    def round_back(rows):
        for j in range(3 * GROUPS):
            low = dqkv[j, rows].astype(BF)
            dqb[rows, j * LANES : (j + 1) * LANES] = low
            if j < GROUPS:
                add_vec(V_BQ, col_sum(low.astype(F32)), j * LANES)
            elif j >= 2 * GROUPS:
                add_vec(V_BV, col_sum(low.astype(F32)), (j - 2 * GROUPS) * LANES)

    chunks(round_back)
    gqkv_ref[...] += dg(nm[...], dqb[...], TN)
    tmp[...] = dg(dqb[...], wqkv_ref[...], NT)

    def back_one(rows, u, a):
        gn = tmp[rows].astype(BF).astype(F32)
        n, inv = stats(load_cells(tokb, u, a))
        add_vec(V_G1, col_sum(gn * n))
        add_vec(V_B1, col_sum(gn))
        e = gn * vec(V_G1)
        g = ght[rows] + inv * (
            e - jnp.mean(e, axis=-1, keepdims=True) - n * jnp.mean(e * n, axis=-1, keepdims=True)
        )
        gtb[slot, u, a] = g.reshape(WIN, canv, D)

    cell_rows(back_one)
    begin(3, gtok_hbm, gtb, step, slot)

    @pl.when(step + 1 == steps)
    def _():
        for back in (1, 0):
            finish(2, out_hbm, outb, step - back, slot if back == 0 else 1 - slot)
            finish(3, gtok_hbm, gtb, step - back, slot if back == 0 else 1 - slot)
        for ref, base in matrices((gqkv_ref, gout_ref, gup_ref)):
            wide = ref.shape[1] // LANES
            for j in range(wide):
                flat[pl.ds(base + j, D, stride=wide)] = ref[:, j * LANES : (j + 1) * LANES]
        base = D * (3 * D + D + FF) // LANES
        for i in range(FF // LANES):
            for j in range(GROUPS):
                block = gdn_ref[j * LANES : (j + 1) * LANES, i * LANES : (i + 1) * LANES]
                flat[pl.ds(base + i * LANES * GROUPS + j, LANES, stride=GROUPS)] = jnp.transpose(block)
        for row, j, at in vector_rows():
            flat[at : at + 1] = gvec_ref[row : row + 1, j * LANES : (j + 1) * LANES]
        size = send_ref.shape[1]
        for k, start in enumerate(starts):
            send_ref[k] = flat[start : start + size].astype(BF)


VECTORS = (D, D, D, FF, D, D, D, D, D)
P_SIZE = D * (3 * D + D + 2 * FF) + sum(VECTORS)


def matrices(refs):
    base, made = 0, []
    for ref in refs:
        made.append((ref, base))
        base += ref.shape[0] * ref.shape[1] // LANES
    return made


def vector_rows():
    at = D * (3 * D + D + 2 * FF) // LANES
    made = []
    for row, width in enumerate(VECTORS):
        for j in range(width // LANES):
            made.append((row, j, at))
            at += 1
    return made


def part_rows(devices):
    return -(-(P_SIZE // devices + LANES - 1) // LANES // 16) * 16


def block_call(tokens, cot, labels, bias, parts):
    canv = tokens.shape[2]
    rows = PAIR * CELLS * canv
    tall = (PAIR - 1) * CELLS * canv + KEYS * canv
    devices, size = parts.shape[:2]
    share = P_SIZE // devices
    starts = tuple(k * share // LANES for k in range(devices))
    flat_rows = -(-max(starts[-1] + size, P_SIZE // LANES) // 8) * 8
    hbm = pl.BlockSpec(memory_space=pl.ANY)

    def whole(*shape):
        return pl.BlockSpec(shape, lambda i: (0,) * len(shape), pipeline_mode=pl.Buffered(1))

    cells = (2, PAIR, WIN, WIN, canv, D)
    return pl.pallas_call(
        partial(block_kernel, canv, starts),
        grid=(BANDS * BANDS // PAIR,),
        out_shape=[
            jax.ShapeDtypeStruct(tokens.shape, BF),
            jax.ShapeDtypeStruct(tokens.shape, F32),
            jax.ShapeDtypeStruct(parts.shape, BF),
            jax.ShapeDtypeStruct((GROUPS, 2 * KEYS, LANES), F32),
        ],
        in_specs=[
            hbm, hbm,
            pl.BlockSpec((PAIR, canv, LANES), lambda i: (i, 0, 0)),
            whole(GROUPS, 2 * KEYS, LANES),
            hbm,
        ],
        out_specs=[hbm, hbm, whole(*parts.shape), whole(GROUPS, 2 * KEYS, LANES)],
        scratch_shapes=[
            pltpu.VMEM((flat_rows, LANES), F32),
            pltpu.VMEM((D, 3 * D), BF),
            pltpu.VMEM((D, D), BF),
            pltpu.VMEM((D, FF), BF),
            pltpu.VMEM((FF, D), BF),
            pltpu.VMEM((16, FF), F32),
            pltpu.VMEM((D, 3 * D), F32),
            pltpu.VMEM((D, D), F32),
            pltpu.VMEM((D, FF), F32),
            pltpu.VMEM((D, FF), F32),
            pltpu.VMEM((16, FF), F32),
            pltpu.SemaphoreType.DMA,
            pltpu.VMEM(cells, BF),
            pltpu.VMEM(cells, BF),
            pltpu.VMEM(cells, BF),
            pltpu.VMEM(cells, F32),
            pltpu.SemaphoreType.DMA((4, 2, 4 * PAIR)),
            pltpu.VMEM((rows, D), BF),
            pltpu.VMEM((rows, D), BF),
            pltpu.VMEM((3 * GROUPS, tall, LANES), F32),
            pltpu.VMEM((PAIR, canv * GROUPS, 2 * KEYS, LANES), F32),
            pltpu.VMEM((GROUPS, tall, LANES), F32),
            pltpu.VMEM((rows, D), BF),
            pltpu.VMEM((rows, D), F32),
            pltpu.VMEM((rows, D), BF),
            pltpu.VMEM((rows, D), F32),
            pltpu.VMEM((rows, 1), F32),
            pltpu.VMEM((rows, FF), BF),
            pltpu.VMEM((rows, FF), BF),
            pltpu.VMEM((rows, D), F32),
            pltpu.VMEM((rows, D), BF),
            pltpu.VMEM((3 * GROUPS, tall, LANES), F32),
            pltpu.VMEM((rows, 3 * D), BF),
            pltpu.VMEM((rows, D), F32),
            pltpu.VMEM((GROUPS, tall, LANES), F32),
        ],
        compiler_params=pltpu.CompilerParams(vmem_limit_bytes=63 << 20),
        name="block",
    )(tokens, cot, labels, bias, parts)


def split_windows(field):
    canvases, band_rows, columns, channels = field.shape
    field = field.reshape(canvases, band_rows // WIN, WIN, columns // WIN, WIN, channels)
    return field.transpose(0, 1, 3, 2, 4, 5).reshape(-1, WIN * WIN, channels)


def window_labels(crop_ids):
    canvases, height, columns = crop_ids.shape
    crop_roll = jnp.roll(crop_ids, (-SHIFT, -SHIFT), (1, 2))
    row_flag = (jnp.arange(height, dtype=jnp.int32) >= height - SHIFT).astype(jnp.int32)
    col_flag = (jnp.arange(columns, dtype=jnp.int32) >= columns - SHIFT).astype(jnp.int32)
    labels = crop_roll * 4 + 2 * row_flag[None, :, None] + col_flag[None, None, :]
    labels = split_windows(labels[..., None])[:, :, 0].reshape(canvases, -1, CELLS)
    labels = jnp.pad(labels, ((0, 0), (0, 0), (0, 64 - CELLS)), constant_values=-1)
    return jnp.concatenate([labels, labels], axis=-1).astype(F32).transpose(1, 0, 2)


def offset_onehot():
    j, i, t = (lax.broadcasted_iota(jnp.int32, (KEYS, 64, TABLE), k) for k in range(3))
    index = (i // WIN - j // WIN + WIN - 1) * (2 * WIN - 1) + i % WIN - j % WIN + WIN - 1
    live = jnp.logical_and(i < CELLS, j < CELLS)
    return jnp.logical_and(index == t, live).astype(F32)


def pair_bias(table):
    hot = offset_onehot()
    full = jnp.einsum("jit,th->hji", hot, table, precision=lax.Precision.HIGHEST)
    full = full.reshape(GROUPS, 2, 2, KEYS, 64).transpose(0, 2, 3, 1, 4)
    return full.reshape(GROUPS, 2 * KEYS, LANES)


def table_sum(gbias):
    hot = offset_onehot()
    full = gbias.reshape(GROUPS, 2, KEYS, 2, 64).transpose(0, 3, 1, 2, 4).reshape(HEADS, KEYS, 64)
    return jnp.einsum("jit,hji->th", hot, full, precision=lax.Precision.HIGHEST)


def local_block(tokens, crop_ids, parts, bias_table, cotangent):
    out_tokens, grad_tokens, send, gbias = block_call(
        tokens.transpose(1, 2, 0, 3), cotangent.transpose(1, 2, 0, 3), window_labels(crop_ids), pair_bias(bias_table), parts
    )
    return out_tokens.transpose(2, 0, 1, 3), grad_tokens.transpose(2, 0, 1, 3), send, table_sum(gbias)


MESH = pl.DeviceIdType.MESH


class Place:
    def __init__(self, sizes):
        self.A, self.Y = sizes[0] // 2, sizes[1] // 2
        dp, shard = lax.axis_index("dp"), lax.axis_index("shard")
        self.a, self.b = dp // 2, lax.rem(dp, 2)
        self.y, self.c = shard // 2, lax.rem(shard, 2)
        self.dp, self.shard = dp, shard

    def at(self, a=None, b=None, y=None, c=None):
        a, b = self.a if a is None else a, self.b if b is None else b
        y, c = self.y if y is None else y, self.c if c is None else c
        return (a * 2 + b, y * 2 + c)

    def turn_a(self, k):
        return lax.rem(self.a + k, self.A)

    def turn_y(self, k):
        return lax.rem(self.y + k, self.Y)

    def peers(self):
        found = [self.at(b=1 - self.b), self.at(c=1 - self.c)]
        found += [self.at(a=self.turn_a(k)) for k in range(1, self.A)]
        found += [self.at(y=self.turn_y(k)) for k in range(1, self.Y)]
        return found


def greet(peers):
    barrier = pltpu.get_barrier_semaphore()
    for peer in peers:
        pl.semaphore_signal(barrier, inc=1, device_id=peer, device_id_type=MESH)
    pl.semaphore_wait(barrier, len(peers))


def gather_kernel(sizes, mine, all_ref, own_sem, sems):
    me = Place(sizes)
    A, Y = me.A, me.Y
    half = mine.shape[0] // 2
    parts = (pl.ds(0, half), pl.ds(half, half))
    a, b, y, c = me.a, me.b, me.y, me.c
    own = pltpu.make_async_copy(mine, all_ref.at[a, b, y, c], own_sem)
    own.start()
    greet(me.peers())

    def send(kind, k, src, dst, peer):
        copy = pltpu.make_async_remote_copy(
            src_ref=src, dst_ref=dst, send_sem=sems.at[0, kind, k], recv_sem=sems.at[1, kind, k],
            device_id=peer, device_id_type=MESH,
        )
        copy.start()
        return copy

    sent = []
    far = [None]
    for k in range(1, A):
        far.append(send(0, k, mine, all_ref.at[a, b, y, c], me.at(a=lax.rem(a - k + A, A))))
    sent += far[1:]
    own.wait()
    first = []
    for k in range(A):
        if k:
            far[k].wait_recv()
        z = me.turn_a(k)
        xs = send(1, k, all_ref.at[z, b, y, c, parts[0]], all_ref.at[z, b, y, c, parts[0]], me.at(b=1 - b))
        ys, more = [], []
        for j in range(1, Y):
            peer = me.at(y=lax.rem(y - j + Y, Y))
            ys.append(send(2, k * Y + j, all_ref.at[z, b, y, c, parts[1]], all_ref.at[z, b, y, c, parts[1]], peer))
        more.append(send(3, k * Y, all_ref.at[z, b, y, c, parts[1]], all_ref.at[z, b, y, c, parts[1]], me.at(b=1 - b)))
        for j in range(1, Y):
            peer = me.at(y=lax.rem(y - j + Y, Y))
            more.append(send(4, k * Y + j, all_ref.at[z, b, y, c, parts[0]], all_ref.at[z, b, y, c, parts[0]], peer))
        first.append((xs, ys, more))
    last = []
    for k in range(A):
        z = me.turn_a(k)
        xs, ys, more = first[k]
        xs.wait_recv()
        onward = []
        for j in range(1, Y):
            peer = me.at(y=lax.rem(y - j + Y, Y))
            onward.append(
                send(5, k * Y + j, all_ref.at[z, 1 - b, y, c, parts[0]], all_ref.at[z, 1 - b, y, c, parts[0]], peer)
            )
        for j in range(1, Y):
            ys[j - 1].wait_recv()
            w = me.turn_y(j)
            onward.append(
                send(6, k * Y + j, all_ref.at[z, b, w, c, parts[1]], all_ref.at[z, b, w, c, parts[1]], me.at(b=1 - b))
            )
        sent += [xs] + ys + more + onward
        last.append(more + onward)
    ends = []
    for k in range(A):
        z = me.turn_a(k)
        for copy in last[k]:
            copy.wait_recv()
        ends.append(send(7, k, all_ref.at[z, :, :, c], all_ref.at[z, :, :, c], me.at(c=1 - c)))
    for copy in ends:
        copy.wait_recv()
    for copy in sent + ends:
        copy.wait_send()


def gather_call(mesh_sizes, mine):
    A, Y = mesh_sizes[0] // 2, mesh_sizes[1] // 2
    return pl.pallas_call(
        partial(gather_kernel, mesh_sizes),
        out_shape=jax.ShapeDtypeStruct((A, 2, Y, 2) + mine.shape, mine.dtype),
        in_specs=[pl.BlockSpec(memory_space=pltpu.VMEM)],
        out_specs=pl.BlockSpec(memory_space=pl.ANY),
        scratch_shapes=[pltpu.SemaphoreType.DMA, pltpu.SemaphoreType.DMA((2, 8, A * Y))],
        compiler_params=pltpu.CompilerParams(collective_id=0, has_side_effects=True),
        name="gather",
    )(mine)


def scatter_kernel(sizes, share, x_ref, t_ref, sum_ref, tab_ref, sq_ref,
                   b0, y0, bx0, by1, y1h0, y1h1, by0, bx1, y2, bz, tbuf, qbuf, sems, small):
    me = Place(sizes)
    A, Y = me.A, me.Y
    a, b, y, c = me.a, me.b, me.y, me.c
    size = sum_ref.shape[0]
    half = size // 2
    lo, hi = pl.ds(0, half), pl.ds(half, half)
    greet(me.peers())

    def send(kind, k, src, dst, peer):
        copy = pltpu.make_async_remote_copy(
            src_ref=src, dst_ref=dst, send_sem=sems.at[0, kind, k], recv_sem=sems.at[1, kind, k],
            device_id=peer, device_id_type=MESH,
        )
        copy.start()
        return copy

    def small_send(kind, k, src, dst, peer):
        copy = pltpu.make_async_remote_copy(
            src_ref=src, dst_ref=dst, send_sem=small.at[0, kind, k], recv_sem=small.at[1, kind, k],
            device_id=peer, device_id_type=MESH,
        )
        copy.start()
        return copy

    sent = []
    core = []
    for i, rows in enumerate((lo, hi)):
        core.append(send(0, i, x_ref.at[:, :, :, 1 - c, rows], b0.at[i], me.at(c=1 - c)))
    tbuf[0] = t_ref[...]
    t0 = small_send(0, 0, tbuf.at[0], tbuf.at[1], me.at(c=1 - c))
    sent += core + [t0]

    def add(dst, one, two):
        dst[...] = (one.astype(F32) + two.astype(F32)).astype(BF)

    for i, rows in enumerate((lo, hi)):
        core[i].wait_recv()

        def over_a(k, carry, i=i, rows=rows):
            for p in range(2):
                for q in range(Y):
                    add(y0.at[i, k, p, q], x_ref[k, p, q, c, rows], b0[i, k, p, q])
            return carry

        lax.fori_loop(0, A, over_a, 0)
        if i == 0:
            xs = send(1, 0, y0.at[0, :, 1 - b], bx0, me.at(b=1 - b))
        else:
            ys = []
            for j in range(1, Y):
                peer = lax.rem(y - j + Y, Y)
                ys.append(send(2, j, y0.at[1, :, :, peer], by1.at[j - 1], me.at(y=peer)))
    t0.wait_recv()
    tbuf[2] = tbuf[0] + tbuf[1]
    t1 = small_send(1, 0, tbuf.at[2], tbuf.at[3], me.at(b=1 - b))
    sent += [xs, t1] + ys
    xs.wait_recv()

    def low_second(k, carry):
        for q in range(Y):
            add(y1h0.at[k, q], y0[0, k, b, q], bx0[k, q])
        return carry

    lax.fori_loop(0, A, low_second, 0)
    ys2 = []
    for j in range(1, Y):
        peer = lax.rem(y - j + Y, Y)
        ys2.append(send(3, j, y1h0.at[:, peer], by0.at[j - 1], me.at(y=peer)))
    for copy in ys:
        copy.wait_recv()

    def high_second(k, carry):
        for p in range(2):
            total = y0[1, k, p, y].astype(F32)
            for j in range(1, Y):
                total = total + by1[j - 1, k, p].astype(F32)
            y1h1[k, p] = total.astype(BF)
        return carry

    lax.fori_loop(0, A, high_second, 0)
    xs2 = send(4, 0, y1h1.at[:, 1 - b], bx1, me.at(b=1 - b))
    t1.wait_recv()
    tbuf[4 + y] = tbuf[2] + tbuf[3]
    t2 = []
    for j in range(1, Y):
        t2.append(small_send(2, j, tbuf.at[4 + y], tbuf.at[4 + y], me.at(y=lax.rem(y - j + Y, Y))))
    sent += ys2 + [xs2] + t2
    for copy in ys2:
        copy.wait_recv()

    def low_third(k, carry):
        total = y1h0[k, y].astype(F32)
        for j in range(1, Y):
            total = total + by0[j - 1, k].astype(F32)
        y2[k, lo] = total.astype(BF)
        return carry

    lax.fori_loop(0, A, low_third, 0)
    xs2.wait_recv()

    def high_third(k, carry):
        add(y2.at[k, hi], y1h1[k, b], bx1[k])
        return carry

    lax.fori_loop(0, A, high_third, 0)
    zs = []
    for k in range(1, A):
        peer = lax.rem(a - k + A, A)
        zs.append(send(5, k, y2.at[peer], bz.at[k - 1], me.at(a=peer)))
    for copy in t2:
        copy.wait_recv()
    total = tbuf[4]
    for j in range(1, Y):
        total = total + tbuf[4 + j]
    tbuf[4 + Y + a] = total
    t3 = []
    for k in range(1, A):
        t3.append(small_send(3, k, tbuf.at[4 + Y + a], tbuf.at[4 + Y + a], me.at(a=lax.rem(a - k + A, A))))
    sent += zs + t3
    for copy in zs:
        copy.wait_recv()
    total = y2[a].astype(F32)
    for k in range(1, A):
        total = total + bz[k - 1].astype(F32)
    sum_ref[...] = total
    offset = lax.rem((me.dp * (2 * Y) + me.shard) * share, LANES)
    place = lax.broadcasted_iota(jnp.int32, (size, LANES), 0) * LANES + lax.broadcasted_iota(jnp.int32, (size, LANES), 1)
    live = jnp.logical_and(place >= offset, place < offset + share)
    squares = jnp.where(live, total * total, 0.0).reshape(size // 8, 8, LANES)
    squares = jnp.sum(squares, axis=0)
    S, G = 2 * Y, 2 * A
    qbuf[me.shard] = squares
    q0 = []
    for k in range(1, S):
        peer = (me.dp, lax.rem(me.shard - k + S, S))
        q0.append(small_send(4, k, qbuf.at[me.shard], qbuf.at[me.shard], peer))
    for copy in q0:
        copy.wait_recv()
    part = qbuf[0]
    for k in range(1, S):
        part = part + qbuf[k]
    qbuf[S + me.dp] = part
    q1 = []
    for k in range(1, G):
        peer = (lax.rem(me.dp - k + G, G), me.shard)
        q1.append(small_send(5, k, qbuf.at[S + me.dp], qbuf.at[S + me.dp], peer))
    for copy in q1:
        copy.wait_recv()
    part = qbuf[S]
    for k in range(1, G):
        part = part + qbuf[S + k]
    sq_ref[...] = part
    for copy in t3:
        copy.wait_recv()
    total = tbuf[4 + Y]
    for k in range(1, A):
        total = total + tbuf[4 + Y + k]
    tab_ref[...] = total
    for copy in sent + q0 + q1:
        copy.wait_send()


def scatter_call(mesh_sizes, share, x, table):
    A, Y = mesh_sizes[0] // 2, mesh_sizes[1] // 2
    size = x.shape[-2]
    half = size // 2
    vmem = pl.BlockSpec(memory_space=pltpu.VMEM)
    widest = max(2 * A, 2 * Y)
    return pl.pallas_call(
        partial(scatter_kernel, mesh_sizes, share),
        out_shape=[
            jax.ShapeDtypeStruct((size, LANES), F32),
            jax.ShapeDtypeStruct((16, LANES), F32),
            jax.ShapeDtypeStruct((8, LANES), F32),
        ],
        in_specs=[vmem, vmem],
        out_specs=[vmem, vmem, vmem],
        scratch_shapes=[
            pltpu.VMEM((2, A, 2, Y, half, LANES), BF),
            pltpu.VMEM((2, A, 2, Y, half, LANES), BF),
            pltpu.VMEM((A, Y, half, LANES), BF),
            pltpu.VMEM((max(Y - 1, 1), A, 2, half, LANES), BF),
            pltpu.VMEM((A, Y, half, LANES), BF),
            pltpu.VMEM((A, 2, half, LANES), BF),
            pltpu.VMEM((max(Y - 1, 1), A, half, LANES), BF),
            pltpu.VMEM((A, half, LANES), BF),
            pltpu.VMEM((A, size, LANES), BF),
            pltpu.VMEM((max(A - 1, 1), size, LANES), BF),
            pltpu.VMEM((4 + Y + A, 16, LANES), F32),
            pltpu.VMEM((2 * Y + 2 * A, 8, LANES), F32),
            pltpu.SemaphoreType.DMA((2, 6, widest)),
            pltpu.SemaphoreType.DMA((2, 6, widest)),
        ],
        compiler_params=pltpu.CompilerParams(
            collective_id=1, has_side_effects=True, vmem_limit_bytes=60 << 20
        ),
        name="scatter",
    )(x, table)


LEARN_RATE = 0.1
BETA_ONE = 0.9
BETA_TWO = 0.999
ADAM_EPS = 1e-08
WEIGHT_DECAY = 0.05
MAX_NORM = 1.0


def adamw(weights, gradient, first_old, second_old):
    first_new = BETA_ONE * first_old + (1.0 - BETA_ONE) * gradient
    second_new = BETA_TWO * second_old + (1.0 - BETA_TWO) * gradient * gradient
    first_hat = first_new / (1.0 - BETA_ONE**STEP)
    second_hat = second_new / (1.0 - BETA_TWO**STEP)
    updated = weights - LEARN_RATE * (first_hat / (jnp.sqrt(second_hat) + ADAM_EPS) + WEIGHT_DECAY * weights)
    return (updated, first_new, second_new)


def local(
    sizes, tokens, crop_ids, params, first_moment, second_moment, bias_table, table_first, table_second, cotangent
):
    devices = sizes[0] * sizes[1]
    share = params.shape[0]
    size = part_rows(devices)
    offset = lax.rem((lax.axis_index("dp") * sizes[1] + lax.axis_index("shard")) * share, LANES)
    mine = lax.dynamic_update_slice(jnp.zeros((size * LANES,), F32), params, (offset,))
    parts = gather_call(sizes, mine.reshape(size, LANES).astype(BF))
    digits = parts.shape
    out_tokens, grad_tokens, send, g_table = local_block(
        tokens, crop_ids, parts.reshape(devices, size, LANES), bias_table, cotangent
    )
    flat_table = jnp.pad(g_table.reshape(-1), (0, 16 * LANES - g_table.size)).reshape(16, LANES)
    total, table_total, squares = scatter_call(sizes, share, send.reshape(digits), flat_table)
    grad_shard = lax.dynamic_slice(total.reshape(-1), (offset,), (share,))
    table_grad = table_total.reshape(-1)[: g_table.size].reshape(g_table.shape)
    grad_norm = jnp.sqrt(jnp.sum(squares) + jnp.sum(table_grad * table_grad))
    factor = jnp.minimum(1.0, MAX_NORM / (grad_norm + 1e-06))
    new_params, new_first, new_second = adamw(params, grad_shard * factor, first_moment, second_moment)
    new_table, new_table_first, new_table_second = adamw(bias_table, table_grad * factor, table_first, table_second)
    return (
        out_tokens, grad_tokens, grad_shard, table_grad, grad_norm, new_params, new_first, new_second,
        new_table, new_table_first, new_table_second,
    )


def solution(mesh):
    both = P(("dp", "shard"))
    return jax.shard_map(
        partial(local, (mesh.shape["dp"], mesh.shape["shard"])),
        mesh=mesh,
        in_specs=(both, both, both, both, both, P(), P(), P(), both),
        out_specs=(both, both, both, P(), P(), both, both, both, P(), P(), P()),
        check_vma=False,
    )
```

```python
from functools import partial
import math

import jax
import jax.numpy as jnp
import numpy as np
from jax import lax
from jax.experimental import pallas as pl
from jax.experimental.pallas import tpu as pltpu
from jax.sharding import PartitionSpec as P

D = 384
HEADS = 12
HDIM = 32
FF = 1536
WIN = 7
CELLS = WIN * WIN
SHIFT = 3
STEP = 10
TABLE = 169
ROWS = 28
BANDS = ROWS // WIN
TOK = ROWS * ROWS
BAND = WIN * ROWS
STRIDE = 8
PAIR = 2
GROUPS = 3
KEYS = 56
LANES = 128
NORM_EPS = 1e-05
SCALE = HDIM**-0.5
BF = jnp.bfloat16
F32 = jnp.float32
NN = (((1,), (0,)), ((), ()))
NT = (((1,), (1,)), ((), ()))
TN = (((0,), (0,)), ((), ()))
CHUNK = 784

V_BQ, V_BV, V_BO, V_BUP, V_BDN, V_G1, V_B1, V_G2, V_B2 = range(9)


def dg(a, b, dims):
    return lax.dot_general(a, b, dims, preferred_element_type=F32)


def lanes_iota(rows):
    return lax.broadcasted_iota(jnp.int32, (rows, LANES), 1)


def split_keys(block):
    odd = (lanes_iota(KEYS) // HDIM) % 2 == 1
    return jnp.concatenate([jnp.where(odd, 0.0, block), jnp.where(odd, block, 0.0)], axis=0).astype(BF)


def join_keys(both):
    odd = (lanes_iota(KEYS) // HDIM) % 2 == 1
    return jnp.where(odd, both[KEYS:], both[:KEYS])


def split_queries(block):
    high = lanes_iota(KEYS) >= 64
    live = lax.broadcasted_iota(jnp.int32, (KEYS, LANES), 0) < CELLS
    zero = jnp.zeros((8, LANES), F32)
    low_part = jnp.where(jnp.logical_and(live, jnp.logical_not(high)), block, 0.0)
    high_part = jnp.where(jnp.logical_and(live, high), block, 0.0)
    return jnp.concatenate([low_part, zero, high_part, zero], axis=0).astype(BF)


def corner(one, two):
    upper = jnp.concatenate([one, jnp.zeros_like(two)], axis=1)
    lower = jnp.concatenate([jnp.zeros_like(one), two], axis=1)
    return jnp.concatenate([upper, lower], axis=0)


def join_queries(both):
    high = lanes_iota(KEYS) >= 64
    return jnp.where(high, both[64 : 64 + KEYS], both[:KEYS])


def block_kernel(
    canv, starts, tok_hbm, cot_hbm, lab_ref, spread_ref, parts_hbm,
    out_hbm, gtok_hbm, send_ref, gspread_ref,
    big, wqkv_ref, wout_ref, wup_ref, wdn_ref, vec_ref, gqkv_ref, gout_ref, gup_ref, gdn_ref, gvec_ref, parts_sem,
    tokb, cotb, outb, gtb, sems,
    cotw, nm, prob, mix, mixb, hid, nt, n2, inv2, act, gup_act, ght, gab, dqb, tmp, tmp3, rest, q2s, k2s, v2s, bias_ref, gbias_ref,
):
    step = pl.program_id(0)
    steps = pl.num_programs(0)
    slot = lax.rem(step, 2)
    wrows = CELLS * canv
    rows_all = PAIR * wrows
    tall = rows_all + (KEYS - CELLS) * canv
    flat = big
    qkv = [big.at[pl.ds(j * tall, tall)] for j in range(3 * GROUPS)]
    dqkv = [big.at[pl.ds((3 * GROUPS + j) * tall, tall)] for j in range(3 * GROUPS)]
    mix = [mix.at[j] for j in range(GROUPS)]
    tmp3 = [tmp3.at[j] for j in range(GROUPS)]

    def copies(kind, hbm, buf, at, where):
        made = []
        for u in range(PAIR):
            w = at * PAIR + u
            wr, wc = w // BANDS, lax.rem(w, BANDS)
            for ra, rn in ((0, 4), (4, 3)):
                r0 = lax.rem(WIN * wr + SHIFT + ra, ROWS)
                for ca, cn in ((0, 4), (4, 3)):
                    c0 = lax.rem(WIN * wc + SHIFT + ca, ROWS)
                    far = hbm.at[pl.ds(r0, rn), pl.ds(c0, cn)]
                    near = buf.at[where, u, pl.ds(ra, rn), pl.ds(ca, cn)]
                    sem = sems.at[kind, where, len(made)]
                    made.append(
                        pltpu.make_async_copy(far, near, sem) if kind < 2 else pltpu.make_async_copy(near, far, sem)
                    )
        return made

    def begin(*what):
        for copy in copies(*what):
            copy.start()

    def finish(*what):
        for copy in copies(*what):
            copy.wait()

    @pl.when(step == 0)
    def _():
        gathered = pltpu.make_async_copy(parts_hbm, send_ref, parts_sem)
        gathered.start()
        begin(0, tok_hbm, tokb, step, slot)
        begin(1, cot_hbm, cotb, step, slot)
        for ref in (gqkv_ref, gout_ref, gup_ref, gdn_ref, gvec_ref, gbias_ref):
            ref[...] = jnp.zeros_like(ref)
        for g in range(GROUPS):
            for h in range(2):
                bias_ref[g, h * KEYS : (h + 1) * KEYS] = spread_ref[pl.ds(2 * g + h, KEYS, stride=8)]
        gathered.wait()
        flat[:8] = jnp.zeros((8, LANES), F32)
        for k, start in enumerate(starts):
            part = send_ref[k].astype(F32)
            first = part[:8] + jnp.where(lax.broadcasted_iota(jnp.int32, (8, LANES), 0) == 0, flat[start : start + 8], 0.0)
            flat[start : start + 8] = first
            flat[start + 8 : start + part.shape[0]] = part[8:]
        for ref, base in matrices((wqkv_ref, wout_ref, wup_ref, wdn_ref)):
            wide = ref.shape[1] // LANES
            for j in range(wide):
                ref[:, j * LANES : (j + 1) * LANES] = flat[pl.ds(base + j, ref.shape[0], stride=wide)].astype(BF)
        for row, j, at in vector_rows():
            vec_ref[row : row + 1, j * LANES : (j + 1) * LANES] = flat[at : at + 1]
        for ref in qkv + tmp3:
            ref[rows_all:] = jnp.zeros((tall - rows_all, LANES), F32)

    @pl.when(step + 1 < steps)
    def _():
        begin(0, tok_hbm, tokb, step + 1, 1 - slot)
        begin(1, cot_hbm, cotb, step + 1, 1 - slot)

    finish(0, tok_hbm, tokb, step, slot)
    finish(1, cot_hbm, cotb, step, slot)

    @pl.when(step >= 2)
    def _():
        finish(2, out_hbm, outb, step - 2, slot)
        finish(3, gtok_hbm, gtb, step - 2, slot)

    extra = rows_all % 256
    main = rows_all - extra
    widths = {"nm": D, "mixb": D, "nt": D, "cotw": D, "gab": D, "dqb": 3 * D, "act": FF, "gup": FF}
    places, at = {}, 0
    for key, width in widths.items():
        places[key] = (at, width)
        at += width

    def keep(key, ref):
        at, width = places[key]
        rest[pl.ds(pl.multiple_of(step * extra, 16), extra), at : at + width] = ref[main:]

    def kept(key, cols=slice(None)):
        at, width = places[key]
        return rest[:, at : at + width][:, cols]

    def vec(row, width=D):
        return vec_ref[row : row + 1, :width]

    def add_vec(row, value, start=0):
        width = value.shape[1]
        gvec_ref[row : row + 1, start : start + width] += value

    def col_sum(value):
        return jnp.sum(value, axis=0, keepdims=True)

    def window_rows(body):
        def one(u, carry):
            body(pl.ds(pl.multiple_of(u * wrows, 8), wrows), u)
            return carry

        for u in range(PAIR):
            one(u, 0)

    def chunks(body):
        body(slice(0, rows_all))

    def stats(x):
        center = x - jnp.mean(x, axis=-1, keepdims=True)
        inv = lax.rsqrt(jnp.mean(center * center, axis=-1, keepdims=True) + NORM_EPS)
        return center * inv, inv

    def load_cells(buf, u):
        return buf[slot, u].astype(F32).reshape(wrows, D)

    def norm_one(rows, u):
        x = load_cells(tokb, u)
        n1, _ = stats(x)
        nm[rows] = (n1 * vec(V_G1) + vec(V_B1)).astype(BF)
        cotw[rows] = load_cells(cotb, u).astype(BF)
        hid[rows] = x

    window_rows(norm_one)

    project = dg(nm[...], wqkv_ref[...], NN)
    for j in range(3):
        part = project[:, j * D : (j + 1) * D]
        if j == 0:
            part = part + vec(V_BQ)
        if j == 2:
            part = part + vec(V_BV)
        for g in range(GROUPS):
            qkv[j * GROUPS + g][:rows_all] = part[:, g * LANES : (g + 1) * LANES]

    UNROLL = 2

    def view(ref, which, u):
        return ref[which].at[pl.ds(pl.multiple_of(u * wrows, 8), KEYS * canv)]

    def take(ref, which, u, c):
        return view(ref, which, u)[pl.ds(c, KEYS, stride=canv)]

    def put(ref, which, u, c, value):
        view(ref, which, u)[pl.ds(c, CELLS, stride=canv)] = value[:CELLS]

    batches = [(u, tuple(range(v, v + UNROLL))) for u in range(PAIR) for v in range(0, canv, UNROLL)]

    def in_turn(*stages):
        held = {}
        for n in range(len(batches) + len(stages) - 1):
            for k, stage in enumerate(stages):
                if 0 <= n - k < len(batches):
                    held[n - k] = stage(*batches[n - k], held.get(n - k))

    def score(u, cs, _):
        raw = {}
        for c in cs:
            for g in range(GROUPS):
                q2 = split_queries(take(qkv, g, u, c) * SCALE)
                k2 = split_keys(take(qkv, GROUPS + g, u, c))
                raw[c, g] = dg(k2, q2, NT)
                q2s[u, c * GROUPS + g] = q2
                k2s[u, c * GROUPS + g] = k2
        return raw

    def soften(u, cs, raw):
        probs = {}
        for c in cs:
            row = lab_ref[u, c : c + 1, :]
            col = jnp.transpose(jnp.broadcast_to(row, (LANES, LANES)))[:KEYS]
            mask = (col == row)[None]
            for g in range(GROUPS):
                s = jnp.where(mask, raw[c, g].reshape(2, KEYS, LANES), -1e30)
                s = s + bias_ref[g].reshape(2, KEYS, LANES)
                e = jnp.exp(s - jnp.max(s, axis=1, keepdims=True))
                p = e * (1.0 / jnp.sum(e, axis=1, keepdims=True))
                probs[c, g] = p.reshape(2 * KEYS, LANES).astype(BF)
                prob[u, c * GROUPS + g] = probs[c, g]
        for c in cs[::2]:
            for g in range(GROUPS):
                v2 = [split_keys(take(qkv, 2 * GROUPS + g, u, d)) for d in (c, c + 1)]
                p = jnp.concatenate([probs[c, g], probs[c + 1, g]], axis=0)
                for d in (0, 1):
                    v2s[u, (c + d) * GROUPS + g] = v2[d]
                o = dg(p, corner(*v2), TN)
                put(mix, g, u, c, join_queries(o[:, :LANES]))
                put(mix, g, u, c + 1, join_queries(o[:, LANES:]))

    in_turn(score, soften)

    for g in range(GROUPS):
        mixb[:, g * LANES : (g + 1) * LANES] = mix[g][:rows_all].astype(BF)
    hid[...] += dg(mixb[...], wout_ref[...], NN) + vec(V_BO)

    def norm_two(rows):
        n, inv = stats(hid[rows])
        n2[rows] = n
        inv2[rows] = inv
        nt[rows] = (n * vec(V_G2) + vec(V_B2)).astype(BF)

    chunks(norm_two)

    FC = 768
    for f in range(FF // FC):
        cols = slice(f * FC, (f + 1) * FC)
        up = dg(nt[...], wup_ref[:, cols], NN) + vec_ref[V_BUP : V_BUP + 1, cols]
        dact = dg(cotw[...], wdn_ref[cols, :], NT)
        cdf = 0.5 + 0.5 * lax.erf(up * (0.5**0.5))
        act[:, cols] = (up * cdf).astype(BF)
        slope = cdf + up * (jnp.exp(-0.5 * up * up) * (1.0 / math.sqrt(2.0 * math.pi)))
        gu = (dact * slope).astype(BF)
        gup_act[:, cols] = gu
        add_vec(V_BUP, col_sum(gu.astype(F32)), f * FC)
    tmp[...] = hid[...] + dg(act[...], wdn_ref[...], NN) + vec(V_BDN)

    def store_out(rows, u):
        outb[slot, u] = tmp[rows].reshape(WIN, WIN, canv, D).astype(BF)

    window_rows(store_out)
    begin(2, out_hbm, outb, step, slot)
    tmp[...] = dg(gup_act[...], wup_ref[...], NT)

    def back_two(rows):
        gn = tmp[rows]
        n = n2[rows]
        c = cotw[rows].astype(F32)
        add_vec(V_G2, col_sum(gn * n))
        add_vec(V_B2, col_sum(gn))
        add_vec(V_BDN, col_sum(c))
        e = gn * vec(V_G2)
        g = c + inv2[rows] * (
            e - jnp.mean(e, axis=-1, keepdims=True) - n * jnp.mean(e * n, axis=-1, keepdims=True)
        )
        ght[rows] = g
        low = g.astype(BF)
        gab[rows] = low
        add_vec(V_BO, col_sum(low.astype(F32)))

    chunks(back_two)
    for f in range(FF // FC):
        cols = slice(f * FC, (f + 1) * FC)
        gup_ref[:, cols] += dg(nt[:main], gup_act[:main, cols], TN)
        gdn_ref[:, cols] += dg(cotw[:main], act[:main, cols], TN)

    part = dg(gab[...], wout_ref[...], NT)
    for g in range(GROUPS):
        tmp3[g][:rows_all] = part[:, g * LANES : (g + 1) * LANES]

    gout_ref[...] += dg(mixb[:main], gab[:main], TN)
    def back_probs(u, cs, _):
        raw, o_of = {}, {}
        for c in cs:
            for g in range(GROUPS):
                v2 = v2s[u, c * GROUPS + g]
                o_of[c, g] = split_queries(take(tmp3, g, u, c))
                raw[c, g] = dg(v2, o_of[c, g], NT)
        return raw, o_of

    def back_rest(u, cs, got):
        raw, o_of = got
        p_of, ds_of = {}, {}

        def side(table, c, g, axis):
            return jnp.concatenate([table[c, g], table[c + 1, g]], axis=axis)

        for c in cs:
            for g in range(GROUPS):
                p_of[c, g] = prob[u, c * GROUPS + g]
                p3 = p_of[c, g].astype(F32).reshape(2, KEYS, LANES)
                dp3 = raw[c, g].reshape(2, KEYS, LANES)
                ds = p3 * (dp3 - jnp.sum(p3 * dp3, axis=1, keepdims=True))
                ds_of[c, g] = ds.reshape(2 * KEYS, LANES).astype(BF)
        for g in range(GROUPS):
            gbias_ref[g] += sum(ds_of[c, g].astype(F32) for c in cs)
        for c in cs[::2]:
            for g in range(GROUPS):
                gv = dg(side(p_of, c, g, 1), corner(o_of[c, g], o_of[c + 1, g]), NN)
                for d in (0, 1):
                    put(dqkv, 2 * GROUPS + g, u, c + d, join_keys(gv[:, d * LANES : (d + 1) * LANES]))
        for c in cs[::2]:
            for g in range(GROUPS):
                q2 = [q2s[u, d * GROUPS + g] for d in (c, c + 1)]
                k2 = [k2s[u, d * GROUPS + g] for d in (c, c + 1)]
                gk = dg(side(ds_of, c, g, 1), corner(*q2), NN)
                gq = dg(side(ds_of, c, g, 0), corner(*k2), TN)
                for d in (0, 1):
                    lanes = slice(d * LANES, (d + 1) * LANES)
                    put(dqkv, g, u, c + d, join_queries(gq[:, lanes]) * SCALE)
                    put(dqkv, GROUPS + g, u, c + d, join_keys(gk[:, lanes]))

    in_turn(back_probs, back_rest)

    def round_back(rows):
        for j in range(3 * GROUPS):
            low = dqkv[j][rows].astype(BF)
            dqb[rows, j * LANES : (j + 1) * LANES] = low
            if j < GROUPS:
                add_vec(V_BQ, col_sum(low.astype(F32)), j * LANES)
            elif j >= 2 * GROUPS:
                add_vec(V_BV, col_sum(low.astype(F32)), (j - 2 * GROUPS) * LANES)

    chunks(round_back)
    tmp[...] = dg(dqb[...], wqkv_ref[...], NT)

    def back_one(rows, u):
        gn = tmp[rows].astype(BF).astype(F32)
        n, inv = stats(load_cells(tokb, u))
        add_vec(V_G1, col_sum(gn * n))
        add_vec(V_B1, col_sum(gn))
        e = gn * vec(V_G1)
        g = ght[rows] + inv * (
            e - jnp.mean(e, axis=-1, keepdims=True) - n * jnp.mean(e * n, axis=-1, keepdims=True)
        )
        gtb[slot, u] = g.reshape(WIN, WIN, canv, D)

    window_rows(back_one)
    gqkv_ref[...] += dg(nm[:main], dqb[:main], TN)
    begin(3, gtok_hbm, gtb, step, slot)
    for key, ref in zip(widths, (nm, mixb, nt, cotw, gab, dqb, act, gup_act)):
        keep(key, ref)

    @pl.when(step + 1 == steps)
    def _():
        gqkv_ref[...] += dg(kept("nm"), kept("dqb"), TN)
        gout_ref[...] += dg(kept("mixb"), kept("gab"), TN)
        gup_ref[...] += dg(kept("nt"), kept("gup"), TN)
        gdn_ref[...] += dg(kept("cotw"), kept("act"), TN)
        for back in (1, 0):
            finish(2, out_hbm, outb, step - back, slot if back == 0 else 1 - slot)
            finish(3, gtok_hbm, gtb, step - back, slot if back == 0 else 1 - slot)
        for ref, base in matrices((gqkv_ref, gout_ref, gup_ref)):
            wide = ref.shape[1] // LANES
            for j in range(wide):
                flat[pl.ds(base + j, D, stride=wide)] = ref[:, j * LANES : (j + 1) * LANES]
        base = D * (3 * D + D + FF) // LANES
        for i in range(FF // LANES):
            for j in range(GROUPS):
                block = gdn_ref[j * LANES : (j + 1) * LANES, i * LANES : (i + 1) * LANES]
                flat[pl.ds(base + i * LANES * GROUPS + j, LANES, stride=GROUPS)] = jnp.transpose(block)
        for row, j, at in vector_rows():
            flat[at : at + 1] = gvec_ref[row : row + 1, j * LANES : (j + 1) * LANES]
        gspread_ref[...] = jnp.zeros_like(gspread_ref)
        for g in range(GROUPS):
            for h in range(2):
                gspread_ref[pl.ds(2 * g + h, KEYS, stride=8)] = gbias_ref[g, h * KEYS : (h + 1) * KEYS]
        size = send_ref.shape[1]
        for k, start in enumerate(starts):
            send_ref[k] = flat[start : start + size].astype(BF)


VECTORS = (D, D, D, FF, D, D, D, D, D)
P_SIZE = D * (3 * D + D + 2 * FF) + sum(VECTORS)


def matrices(refs):
    base, made = 0, []
    for ref in refs:
        made.append((ref, base))
        base += ref.shape[0] * ref.shape[1] // LANES
    return made


def vector_rows():
    at = D * (3 * D + D + 2 * FF) // LANES
    made = []
    for row, width in enumerate(VECTORS):
        for j in range(width // LANES):
            made.append((row, j, at))
            at += 1
    return made


def part_rows(devices):
    return -(-(P_SIZE // devices + LANES - 1) // LANES // 16) * 16


def block_call(tokens, cot, labels, bias, parts):
    canv = tokens.shape[2]
    rows = PAIR * CELLS * canv
    tall = (PAIR - 1) * CELLS * canv + KEYS * canv
    devices, size = parts.shape[:2]
    share = P_SIZE // devices
    starts = tuple(k * share // LANES for k in range(devices))
    flat_rows = -(-max(starts[-1] + size, P_SIZE // LANES) // 8) * 8
    hbm = pl.BlockSpec(memory_space=pl.ANY)

    def whole(*shape):
        return pl.BlockSpec(shape, lambda i: (0,) * len(shape), pipeline_mode=pl.Buffered(1))

    cells = (2, PAIR, WIN, WIN, canv, D)
    return pl.pallas_call(
        partial(block_kernel, canv, starts),
        grid=(BANDS * BANDS // PAIR,),
        out_shape=[
            jax.ShapeDtypeStruct(tokens.shape, BF),
            jax.ShapeDtypeStruct(tokens.shape, F32),
            jax.ShapeDtypeStruct(parts.shape, BF),
            jax.ShapeDtypeStruct((KEYS * 8, LANES), F32),
        ],
        in_specs=[
            hbm, hbm,
            pl.BlockSpec((PAIR, canv, LANES), lambda i: (i, 0, 0)),
            whole(KEYS * 8, LANES),
            hbm,
        ],
        out_specs=[hbm, hbm, whole(*parts.shape), whole(KEYS * 8, LANES)],
        scratch_shapes=[
            pltpu.VMEM((max(flat_rows, 6 * GROUPS * tall), LANES), F32),
            pltpu.VMEM((D, 3 * D), BF),
            pltpu.VMEM((D, D), BF),
            pltpu.VMEM((D, FF), BF),
            pltpu.VMEM((FF, D), BF),
            pltpu.VMEM((16, FF), F32),
            pltpu.VMEM((D, 3 * D), F32),
            pltpu.VMEM((D, D), F32),
            pltpu.VMEM((D, FF), F32),
            pltpu.VMEM((D, FF), F32),
            pltpu.VMEM((16, FF), F32),
            pltpu.SemaphoreType.DMA,
            pltpu.VMEM(cells, BF),
            pltpu.VMEM(cells, BF),
            pltpu.VMEM(cells, BF),
            pltpu.VMEM(cells, F32),
            pltpu.SemaphoreType.DMA((4, 2, 4 * PAIR)),
            pltpu.VMEM((rows, D), BF),
            pltpu.VMEM((rows, D), BF),
            pltpu.VMEM((PAIR, canv * GROUPS, 2 * KEYS, LANES), BF),
            pltpu.VMEM((GROUPS, tall, LANES), F32),
            pltpu.VMEM((rows, D), BF),
            pltpu.VMEM((rows, D), F32),
            pltpu.VMEM((rows, D), BF),
            pltpu.VMEM((rows, D), F32),
            pltpu.VMEM((rows, 1), F32),
            pltpu.VMEM((rows, FF), BF),
            pltpu.VMEM((rows, FF), BF),
            pltpu.VMEM((rows, D), F32),
            pltpu.VMEM((rows, D), BF),
            pltpu.VMEM((rows, 3 * D), BF),
            pltpu.VMEM((rows, D), F32),
            pltpu.VMEM((GROUPS, tall, LANES), F32),
            pltpu.VMEM((BANDS * BANDS // PAIR * (rows % 256), 8 * D + 2 * FF), BF),
            pltpu.VMEM((PAIR, canv * GROUPS, LANES, LANES), BF),
            pltpu.VMEM((PAIR, canv * GROUPS, 2 * KEYS, LANES), BF),
            pltpu.VMEM((PAIR, canv * GROUPS, 2 * KEYS, LANES), BF),
            pltpu.VMEM((GROUPS, 2 * KEYS, LANES), F32),
            pltpu.VMEM((GROUPS, 2 * KEYS, LANES), F32),
        ],
        compiler_params=pltpu.CompilerParams(vmem_limit_bytes=63 << 20),
        name="block",
    )(tokens, cot, labels, bias, parts)


def split_windows(field):
    canvases, band_rows, columns, channels = field.shape
    field = field.reshape(canvases, band_rows // WIN, WIN, columns // WIN, WIN, channels)
    return field.transpose(0, 1, 3, 2, 4, 5).reshape(-1, WIN * WIN, channels)


def window_labels(crop_ids):
    canvases, height, columns = crop_ids.shape
    crop_roll = jnp.roll(crop_ids, (-SHIFT, -SHIFT), (1, 2))
    row_flag = (jnp.arange(height, dtype=jnp.int32) >= height - SHIFT).astype(jnp.int32)
    col_flag = (jnp.arange(columns, dtype=jnp.int32) >= columns - SHIFT).astype(jnp.int32)
    labels = crop_roll * 4 + 2 * row_flag[None, :, None] + col_flag[None, None, :]
    labels = split_windows(labels[..., None])[:, :, 0].reshape(canvases, -1, CELLS)
    labels = jnp.pad(labels, ((0, 0), (0, 0), (0, 64 - CELLS)), constant_values=-1)
    return jnp.concatenate([labels, labels], axis=-1).astype(F32).transpose(1, 0, 2)


def by_pairs(table):
    rows = table.T.reshape(GROUPS, 2, 2, TABLE).transpose(1, 0, 2, 3).reshape(2, 2 * GROUPS, TABLE)
    return jnp.pad(rows, ((0, 0), (0, 2), (0, 176 - TABLE))).reshape(16, 176)


def from_pairs(rows):
    rows = rows[:, :TABLE].reshape(2, 8, TABLE)[:, : 2 * GROUPS].reshape(2, GROUPS, 2, TABLE)
    return rows.transpose(1, 0, 2, 3).reshape(HEADS, TABLE).T


def local_block(tokens, crop_ids, parts, spread, cotangent):
    out_tokens, grad_tokens, send, gspread = block_call(
        tokens.transpose(1, 2, 0, 3), cotangent.transpose(1, 2, 0, 3), window_labels(crop_ids),
        spread.reshape(KEYS * 8, LANES), parts
    )
    return out_tokens.transpose(2, 0, 1, 3), grad_tokens.transpose(2, 0, 1, 3), send, gspread.reshape(KEYS, 8, LANES)


MESH = pl.DeviceIdType.MESH


class Place:
    def __init__(self, sizes):
        self.A, self.Y = sizes[0] // 2, sizes[1] // 2
        dp, shard = lax.axis_index("dp"), lax.axis_index("shard")
        self.a, self.b = dp // 2, lax.rem(dp, 2)
        self.y, self.c = shard // 2, lax.rem(shard, 2)
        self.dp, self.shard = dp, shard

    def at(self, a=None, b=None, y=None, c=None):
        a, b = self.a if a is None else a, self.b if b is None else b
        y, c = self.y if y is None else y, self.c if c is None else c
        return (a * 2 + b, y * 2 + c)

    def turn_a(self, k):
        return lax.rem(self.a + k, self.A)

    def turn_y(self, k):
        return lax.rem(self.y + k, self.Y)

    def peers(self):
        found = [self.at(b=1 - self.b), self.at(c=1 - self.c)]
        found += [self.at(a=self.turn_a(k)) for k in range(1, self.A)]
        found += [self.at(y=self.turn_y(k)) for k in range(1, self.Y)]
        return found


def greet(peers):
    barrier = pltpu.get_barrier_semaphore()
    for peer in peers:
        pl.semaphore_signal(barrier, inc=1, device_id=peer, device_id_type=MESH)
    pl.semaphore_wait(barrier, len(peers))


def offset_hot(rj, cj, width):
    i = lax.rem(lax.broadcasted_iota(jnp.int32, (1, LANES), 1), 64)
    index = (i // WIN) * (2 * WIN - 1) + lax.rem(i, WIN) + TABLE // 2 - (rj * (2 * WIN - 1) + cj)
    index = jnp.where(i < CELLS, index, -1)
    hot = lax.broadcasted_iota(jnp.int32, (width, LANES), 0) == index
    return jnp.where(hot, 1.0, 0.0).astype(BF)


def three_parts(value):
    high = value.astype(BF)
    rest = value - high.astype(F32)
    middle = rest.astype(BF)
    return jnp.concatenate([high, middle, (rest - middle.astype(F32)).astype(BF)], axis=0)


def three_sum(value):
    return value[:16] + value[16:32] + value[32:]


def spread_table(table_ref, bias_ref):
    parts = three_parts(table_ref[...])
    low = lax.broadcasted_iota(jnp.int32, (8, LANES), 1) < 64

    def over(rj, carry):
        for cj in range(WIN):
            got = three_sum(dg(parts, offset_hot(rj, cj, table_ref.shape[1]), NN))
            bias_ref[rj * WIN + cj] = jnp.where(low, got[:8], got[8:])
        return carry

    lax.fori_loop(0, WIN, over, 0)
    bias_ref[CELLS:] = jnp.zeros((KEYS - CELLS, 8, LANES), F32)


def fold_table(bias_ref, width):
    low = lax.broadcasted_iota(jnp.int32, (8, LANES), 1) < 64

    def over(rj, total):
        for cj in range(WIN):
            block = bias_ref[rj * WIN + cj]
            both = jnp.concatenate([jnp.where(low, block, 0.0), jnp.where(low, 0.0, block)], axis=0)
            total = total + dg(three_parts(both), offset_hot(rj, cj, width), NT)
        return total

    return three_sum(lax.fori_loop(0, WIN, over, jnp.zeros((48, width), F32)))


def gather_kernel(sizes, mine, table_ref, all_ref, bias_ref, own_sem, sems):
    me = Place(sizes)
    A, Y = me.A, me.Y
    half = mine.shape[0] // 2
    parts = (pl.ds(0, half), pl.ds(half, half))
    a, b, y, c = me.a, me.b, me.y, me.c
    own = pltpu.make_async_copy(mine, all_ref.at[a, b, y, c], own_sem)
    own.start()
    greet(me.peers())

    def send(kind, k, src, dst, peer):
        copy = pltpu.make_async_remote_copy(
            src_ref=src, dst_ref=dst, send_sem=sems.at[0, kind, k], recv_sem=sems.at[1, kind, k],
            device_id=peer, device_id_type=MESH,
        )
        copy.start()
        return copy

    far = [None]
    for k in range(1, A):
        far.append(send(0, k, mine, all_ref.at[a, b, y, c], me.at(a=lax.rem(a - k + A, A))))
    sent = far[1:]
    ys_peer = [me.at(y=lax.rem(y - j + Y, Y)) for j in range(Y)]
    x_peer, c_peer = me.at(b=1 - b), me.at(c=1 - c)
    state = {}

    def same(kind, k, where, peer):
        return send(kind, k, all_ref.at[where], all_ref.at[where], peer)

    def spread(k):
        if k:
            far[k].wait_recv()
        z = me.turn_a(k)
        lo, hi = (z, b, y, c, parts[0]), (z, b, y, c, parts[1])
        xs = same(1, k, lo, x_peer)
        ys = [same(2, k * Y + j, hi, ys_peer[j]) for j in range(1, Y)]
        more = [same(3, k * Y, hi, x_peer)] + [same(4, k * Y + j, lo, ys_peer[j]) for j in range(1, Y)]
        state[k] = (xs, ys, more)

    def onward(k):
        z = me.turn_a(k)
        xs, ys, more = state[k]
        xs.wait_recv()
        for j in range(1, Y):
            more.append(same(5, k * Y + j, (z, 1 - b, y, c, parts[0]), ys_peer[j]))
        for j in range(1, Y):
            ys[j - 1].wait_recv()
            more.append(same(6, k * Y + j, (z, b, me.turn_y(j), c, parts[1]), x_peer))
        sent.extend([xs] + ys + more)
        state[k] = more

    def across(k):
        z = me.turn_a(k)
        for copy in state[k]:
            copy.wait_recv()
        ends.append(same(7, k, (z, slice(None), slice(None), c), c_peer))

    ends = []
    own.wait()
    for k in range(A + 2):
        if k < A:
            spread(k)
        if k == 0:
            spread_table(table_ref, bias_ref)
        if 0 <= k - 1 < A:
            onward(k - 1)
        if k - 2 >= 0:
            across(k - 2)
    for copy in ends:
        copy.wait_recv()
    for copy in sent + ends:
        copy.wait_send()


def gather_call(mesh_sizes, mine, table):
    A, Y = mesh_sizes[0] // 2, mesh_sizes[1] // 2
    return pl.pallas_call(
        partial(gather_kernel, mesh_sizes),
        out_shape=[
            jax.ShapeDtypeStruct((A, 2, Y, 2) + mine.shape, mine.dtype),
            jax.ShapeDtypeStruct((KEYS, 8, LANES), F32),
        ],
        in_specs=[pl.BlockSpec(memory_space=pltpu.VMEM)] * 2,
        out_specs=[pl.BlockSpec(memory_space=pl.ANY), pl.BlockSpec(memory_space=pltpu.VMEM)],
        scratch_shapes=[pltpu.SemaphoreType.DMA, pltpu.SemaphoreType.DMA((2, 8, A * Y))],
        compiler_params=pltpu.CompilerParams(collective_id=0, has_side_effects=True),
        name="gather",
    )(mine, table)


def scatter_kernel(sizes, share, x_ref, t_ref, sum_ref, tab_ref, norm_ref,
                   b0, y0, bx0, by1, y1h0, y1h1, by0, bx1, y2, bz, tbuf, qbuf, sems, small):
    me = Place(sizes)
    A, Y = me.A, me.Y
    a, b, y, c = me.a, me.b, me.y, me.c
    size = sum_ref.shape[0]
    half = size // 2
    lo, hi = pl.ds(0, half), pl.ds(half, half)
    greet(me.peers())
    sent = []

    def copy_to(table, kind, k, src, dst, peer):
        copy = pltpu.make_async_remote_copy(
            src_ref=src, dst_ref=dst, send_sem=table.at[0, kind, k], recv_sem=table.at[1, kind, k],
            device_id=peer, device_id_type=MESH,
        )
        copy.start()
        sent.append(copy)
        return copy

    send, small_send = partial(copy_to, sems), partial(copy_to, small)
    order = list(range(1, A)) + [0]
    x_peer, c_peer = me.at(b=1 - b), me.at(c=1 - c)
    y_of = [lax.rem(y - j + Y, Y) for j in range(Y)]
    core, first, second, last, tabs = {}, {}, {}, {}, {}
    for k in order:
        core[k] = send(0, k, x_ref.at[me.turn_a(k), :, :, 1 - c], b0.at[k], c_peer)
    tbuf[0] = fold_table(t_ref, tab_ref.shape[1])
    tabs[0] = small_send(0, 0, tbuf.at[0], tbuf.at[1], c_peer)

    def total(*parts):
        out = parts[0].astype(F32)
        for part in parts[1:]:
            out = out + part.astype(F32)
        return out

    def exchange_one(k):
        core[k].wait_recv()
        z = me.turn_a(k)

        def over(i, carry):
            for q in range(Y):
                y0[k, i, q] = total(x_ref[z, i, q, c], b0[k, i, q]).astype(BF)
            return carry

        lax.fori_loop(0, 2, over, 0)
        xs = send(1, k, y0.at[k, 1 - b, :, lo], bx0.at[k], x_peer)
        ys = [send(2, k * Y + j, y0.at[k, :, y_of[j], hi], by1.at[k, j - 1], me.at(y=y_of[j])) for j in range(1, Y)]
        first[k] = (xs, ys)

    def exchange_two(k):
        xs, ys = first[k]
        xs.wait_recv()
        for q in range(Y):
            y1h0[k, q] = total(y0[k, b, q, lo], bx0[k, q]).astype(BF)
        moved = [send(3, k * Y + j, y1h0.at[k, y_of[j]], by0.at[k, j - 1], me.at(y=y_of[j])) for j in range(1, Y)]
        for copy in ys:
            copy.wait_recv()
        for p in range(2):
            y1h1[k, p] = total(y0[k, p, y, hi], *[by1[k, j - 1, p] for j in range(1, Y)]).astype(BF)
        moved.append(send(4, k, y1h1.at[k, 1 - b], bx1.at[k], x_peer))
        second[k] = moved

    def exchange_three(k):
        for copy in second[k]:
            copy.wait_recv()
        low = total(y1h0[k, y], *[by0[k, j - 1] for j in range(1, Y)])
        high = total(y1h1[k, b], bx1[k])
        if k:
            y2[k - 1, lo] = low.astype(BF)
            y2[k - 1, hi] = high.astype(BF)
            last[k] = send(5, k, y2.at[k - 1], bz.at[k - 1], me.at(a=me.turn_a(k)))
        else:
            sum_ref[lo] = low
            sum_ref[hi] = high

    for i in range(A + 2):
        if i < A:
            exchange_one(order[i])
        if i == 0:
            tabs[0].wait_recv()
            tbuf[2] = tbuf[0] + tbuf[1]
            tabs[1] = small_send(1, 0, tbuf.at[2], tbuf.at[3], x_peer)
        if 0 <= i - 1 < A:
            exchange_two(order[i - 1])
        if i == 1:
            tabs[1].wait_recv()
            tbuf[4 + y] = tbuf[2] + tbuf[3]
            tabs[2] = [small_send(2, j, tbuf.at[4 + y], tbuf.at[4 + y], me.at(y=y_of[j])) for j in range(1, Y)]
        if i - 2 >= 0:
            exchange_three(order[i - 2])
        if i == 2:
            for copy in tabs[2]:
                copy.wait_recv()
            tbuf[4 + Y + a] = total(*[tbuf[4 + j] for j in range(Y)])
            tabs[3] = [
                small_send(3, k, tbuf.at[4 + Y + a], tbuf.at[4 + Y + a], me.at(a=lax.rem(a - k + A, A)))
                for k in range(1, A)
            ]
    for k in range(1, A):
        last[k].wait_recv()
    final = total(sum_ref[...], *[bz[k - 1] for k in range(1, A)])
    sum_ref[...] = final
    offset = lax.rem((me.dp * (2 * Y) + me.shard) * share, LANES)
    place = lax.broadcasted_iota(jnp.int32, (size, LANES), 0) * LANES + lax.broadcasted_iota(jnp.int32, (size, LANES), 1)
    live = jnp.logical_and(place >= offset, place < offset + share)
    squares = jnp.where(live, final * final, 0.0).reshape(size // 8, 8, LANES)
    S, G = 2 * Y, 2 * A
    qbuf[me.shard] = jnp.sum(squares, axis=0)
    for copy in [
        small_send(4, k, qbuf.at[me.shard], qbuf.at[me.shard], (me.dp, lax.rem(me.shard - k + S, S))) for k in range(1, S)
    ]:
        copy.wait_recv()
    qbuf[S + me.dp] = total(*[qbuf[k] for k in range(S)])
    round_two = [
        small_send(5, k, qbuf.at[S + me.dp], qbuf.at[S + me.dp], (lax.rem(me.dp - k + G, G), me.shard)) for k in range(1, G)
    ]
    for copy in tabs[3]:
        copy.wait_recv()
    table = total(*[tbuf[4 + Y + k] for k in range(A)])
    tab_ref[...] = table
    table_squares = jnp.sum((table * table).reshape(2, 8, table.shape[1]), axis=0)
    table_squares = table_squares[:, :LANES] + table_squares[:, LANES:]
    for copy in round_two:
        copy.wait_recv()
    both = total(*[qbuf[S + k] for k in range(G)]) + table_squares
    norm = jnp.sqrt(jnp.broadcast_to(jnp.sum(jnp.sum(both, axis=0, keepdims=True), axis=1, keepdims=True), (8, LANES)))
    norm_ref[0:8] = norm
    norm_ref[8:16] = jnp.minimum(1.0, MAX_NORM / (norm + 1e-06))
    for copy in sent:
        copy.wait_send()


def scatter_call(mesh_sizes, share, x, table):
    A, Y = mesh_sizes[0] // 2, mesh_sizes[1] // 2
    size = x.shape[-2]
    half = size // 2
    vmem = pl.BlockSpec(memory_space=pltpu.VMEM)
    widest = max(2 * A, 2 * Y)
    return pl.pallas_call(
        partial(scatter_kernel, mesh_sizes, share),
        out_shape=[
            jax.ShapeDtypeStruct((size, LANES), F32),
            jax.ShapeDtypeStruct((16, 2 * LANES), F32),
            jax.ShapeDtypeStruct((16, LANES), F32),
        ],
        in_specs=[vmem, vmem],
        out_specs=[vmem, vmem, vmem],
        scratch_shapes=[
            pltpu.VMEM((A, 2, Y, size, LANES), BF),
            pltpu.VMEM((A, 2, Y, size, LANES), BF),
            pltpu.VMEM((A, Y, half, LANES), BF),
            pltpu.VMEM((A, Y - 1, 2, half, LANES), BF),
            pltpu.VMEM((A, Y, half, LANES), BF),
            pltpu.VMEM((A, 2, half, LANES), BF),
            pltpu.VMEM((A, Y - 1, half, LANES), BF),
            pltpu.VMEM((A, half, LANES), BF),
            pltpu.VMEM((A - 1, size, LANES), BF),
            pltpu.VMEM((A - 1, size, LANES), BF),
            pltpu.VMEM((4 + Y + A, 16, 2 * LANES), F32),
            pltpu.VMEM((2 * Y + 2 * A, 8, LANES), F32),
            pltpu.SemaphoreType.DMA((2, 6, A * Y)),
            pltpu.SemaphoreType.DMA((2, 6, widest)),
        ],
        compiler_params=pltpu.CompilerParams(
            collective_id=1, has_side_effects=True, vmem_limit_bytes=60 << 20
        ),
        name="scatter",
    )(x, table)


LEARN_RATE = 0.1
BETA_ONE = 0.9
BETA_TWO = 0.999
ADAM_EPS = 1e-08
WEIGHT_DECAY = 0.05
MAX_NORM = 1.0


def adamw(weights, gradient, first_old, second_old):
    first_new = BETA_ONE * first_old + (1.0 - BETA_ONE) * gradient
    second_new = BETA_TWO * second_old + (1.0 - BETA_TWO) * gradient * gradient
    first_hat = first_new / (1.0 - BETA_ONE**STEP)
    second_hat = second_new / (1.0 - BETA_TWO**STEP)
    updated = weights - LEARN_RATE * (first_hat / (jnp.sqrt(second_hat) + ADAM_EPS) + WEIGHT_DECAY * weights)
    return (updated, first_new, second_new)


def local(
    sizes, tokens, crop_ids, params, first_moment, second_moment, bias_table, table_first, table_second, cotangent
):
    devices = sizes[0] * sizes[1]
    share = params.shape[0]
    size = part_rows(devices)
    offset = lax.rem((lax.axis_index("dp") * sizes[1] + lax.axis_index("shard")) * share, LANES)
    mine = lax.dynamic_update_slice(jnp.zeros((size * LANES,), F32), params, (offset,))
    parts, spread = gather_call(sizes, mine.reshape(size, LANES).astype(BF), by_pairs(bias_table))
    digits = parts.shape
    out_tokens, grad_tokens, send, gspread = local_block(
        tokens, crop_ids, parts.reshape(devices, size, LANES), spread, cotangent
    )
    total, table_total, norm = scatter_call(sizes, share, send.reshape(digits), gspread)
    grad_shard = lax.dynamic_slice(total.reshape(-1), (offset,), (share,))
    table_grad = from_pairs(table_total)
    grad_norm, factor = norm[0, 0], norm[8, 0]
    new_params, new_first, new_second = adamw(params, grad_shard * factor, first_moment, second_moment)
    new_table, new_table_first, new_table_second = adamw(bias_table, table_grad * factor, table_first, table_second)
    return (
        out_tokens, grad_tokens, grad_shard, table_grad, grad_norm, new_params, new_first, new_second,
        new_table, new_table_first, new_table_second,
    )


def solution(mesh):
    both = P(("dp", "shard"))
    return jax.shard_map(
        partial(local, (mesh.shape["dp"], mesh.shape["shard"])),
        mesh=mesh,
        in_specs=(both, both, both, both, both, P(), P(), P(), both),
        out_specs=(both, both, both, P(), P(), both, both, both, P(), P(), P()),
        check_vma=False,
    )
```

```python
from functools import partial
import math

import jax
import jax.numpy as jnp
import numpy as np
from jax import lax
from jax.experimental import pallas as pl
from jax.experimental.pallas import tpu as pltpu
from jax.sharding import PartitionSpec as P

D = 384
HEADS = 12
HDIM = 32
FF = 1536
WIN = 7
CELLS = WIN * WIN
SHIFT = 3
STEP = 10
TABLE = 169
ROWS = 28
BANDS = ROWS // WIN
TOK = ROWS * ROWS
BAND = WIN * ROWS
STRIDE = 8
PAIR = 2
GROUPS = 3
KEYS = 56
LANES = 128
NORM_EPS = 1e-05
SCALE = HDIM**-0.5
LOG2E = math.log2(math.e)
BF = jnp.bfloat16
F32 = jnp.float32
NN = (((1,), (0,)), ((), ()))
NT = (((1,), (1,)), ((), ()))
TN = (((0,), (0,)), ((), ()))
CHUNK = 784

V_BQ, V_BV, V_BO, V_BUP, V_BDN, V_G1, V_B1, V_G2, V_B2 = range(9)


def dg(a, b, dims):
    return lax.dot_general(a, b, dims, preferred_element_type=F32)


def lanes_iota(rows):
    return lax.broadcasted_iota(jnp.int32, (rows, LANES), 1)


def split_keys(block):
    odd = (lanes_iota(KEYS) // HDIM) % 2 == 1
    return jnp.concatenate([jnp.where(odd, 0.0, block), jnp.where(odd, block, 0.0)], axis=0).astype(BF)


def join_keys(both):
    odd = (lanes_iota(KEYS) // HDIM) % 2 == 1
    return jnp.where(odd, both[KEYS:], both[:KEYS])


def split_queries(block):
    high = lanes_iota(KEYS) >= 64
    live = lax.broadcasted_iota(jnp.int32, (KEYS, LANES), 0) < CELLS
    zero = jnp.zeros((8, LANES), F32)
    low_part = jnp.where(jnp.logical_and(live, jnp.logical_not(high)), block, 0.0)
    high_part = jnp.where(jnp.logical_and(live, high), block, 0.0)
    return jnp.concatenate([low_part, zero, high_part, zero], axis=0).astype(BF)


def corner(one, two):
    upper = jnp.concatenate([one, jnp.zeros_like(two)], axis=1)
    lower = jnp.concatenate([jnp.zeros_like(one), two], axis=1)
    return jnp.concatenate([upper, lower], axis=0)


def join_queries(both):
    high = lanes_iota(KEYS) >= 64
    return jnp.where(high, both[64 : 64 + KEYS], both[:KEYS])


def block_kernel(
    canv, starts, tok_hbm, cot_hbm, lab_ref, spread_ref, parts_hbm,
    out_hbm, gtok_hbm, send_ref, gspread_ref,
    big, wqkv_ref, wout_ref, wup_ref, wdn_ref, vec_ref, gqkv_ref, gout_ref, gup_ref, gdn_ref, gvec_ref, parts_sem,
    tokb, cotb, outb, gtb, sems,
    cotw, nm, prob, mix, mixb, hid, nt, n2, inv2, act, gup_act, ght, gab, dqb, tmp, tmp3, rest, q2s, k2s, v2s, bias_ref, gbias_ref,
):
    step = pl.program_id(0)
    steps = pl.num_programs(0)
    slot = lax.rem(step, 2)
    wrows = CELLS * canv
    rows_all = PAIR * wrows
    tall = rows_all + (KEYS - CELLS) * canv
    flat = big
    qkv = [big.at[pl.ds(j * tall, tall)] for j in range(3 * GROUPS)]
    dqkv = [big.at[pl.ds((3 * GROUPS + j) * tall, tall)] for j in range(3 * GROUPS)]
    mix = [mix.at[j] for j in range(GROUPS)]
    tmp3 = [tmp3.at[j] for j in range(GROUPS)]

    def copies(kind, hbm, buf, at, where):
        made = []
        for u in range(PAIR):
            w = at * PAIR + u
            wr, wc = w // BANDS, lax.rem(w, BANDS)
            for ra, rn in ((0, 4), (4, 3)):
                r0 = lax.rem(WIN * wr + SHIFT + ra, ROWS)
                for ca, cn in ((0, 4), (4, 3)):
                    c0 = lax.rem(WIN * wc + SHIFT + ca, ROWS)
                    far = hbm.at[pl.ds(r0, rn), pl.ds(c0, cn)]
                    near = buf.at[where, u, pl.ds(ra, rn), pl.ds(ca, cn)]
                    sem = sems.at[kind, where, len(made)]
                    made.append(
                        pltpu.make_async_copy(far, near, sem) if kind < 2 else pltpu.make_async_copy(near, far, sem)
                    )
        return made

    def begin(*what):
        for copy in copies(*what):
            copy.start()

    def finish(*what):
        for copy in copies(*what):
            copy.wait()

    @pl.when(step == 0)
    def _():
        gathered = pltpu.make_async_copy(parts_hbm, send_ref, parts_sem)
        gathered.start()
        begin(0, tok_hbm, tokb, step, slot)
        begin(1, cot_hbm, cotb, step, slot)
        for ref in (gqkv_ref, gout_ref, gup_ref, gdn_ref, gvec_ref, gbias_ref):
            ref[...] = jnp.zeros_like(ref)
        for g in range(GROUPS):
            for h in range(2):
                bias_ref[g, h * KEYS : (h + 1) * KEYS] = spread_ref[pl.ds(2 * g + h, KEYS, stride=8)] * LOG2E
        gathered.wait()
        flat[:8] = jnp.zeros((8, LANES), F32)
        for k, start in enumerate(starts):
            part = send_ref[k].astype(F32)
            first = part[:8] + jnp.where(lax.broadcasted_iota(jnp.int32, (8, LANES), 0) == 0, flat[start : start + 8], 0.0)
            flat[start : start + 8] = first
            flat[start + 8 : start + part.shape[0]] = part[8:]
        for ref, base in matrices((wqkv_ref, wout_ref, wup_ref, wdn_ref)):
            wide = ref.shape[1] // LANES
            for j in range(wide):
                ref[:, j * LANES : (j + 1) * LANES] = flat[pl.ds(base + j, ref.shape[0], stride=wide)].astype(BF)
        for row, j, at in vector_rows():
            vec_ref[row : row + 1, j * LANES : (j + 1) * LANES] = flat[at : at + 1]
        for ref in qkv + tmp3:
            ref[rows_all:] = jnp.zeros((tall - rows_all, LANES), F32)

    @pl.when(step + 1 < steps)
    def _():
        begin(0, tok_hbm, tokb, step + 1, 1 - slot)
        begin(1, cot_hbm, cotb, step + 1, 1 - slot)

    finish(0, tok_hbm, tokb, step, slot)
    finish(1, cot_hbm, cotb, step, slot)

    @pl.when(step >= 2)
    def _():
        finish(2, out_hbm, outb, step - 2, slot)
        finish(3, gtok_hbm, gtb, step - 2, slot)

    extra = rows_all % 256
    main = rows_all - extra
    widths = {"nm": D, "mixb": D, "nt": D, "cotw": D, "gab": D, "dqb": 3 * D, "act": FF, "gup": FF}
    places, at = {}, 0
    for key, width in widths.items():
        places[key] = (at, width)
        at += width

    def keep(key, ref):
        at, width = places[key]
        rest[pl.ds(pl.multiple_of(step * extra, 16), extra), at : at + width] = ref[main:]

    def kept(key, cols=slice(None)):
        at, width = places[key]
        return rest[:, at : at + width][:, cols]

    def vec(row, width=D):
        return vec_ref[row : row + 1, :width]

    def add_vec(row, value, start=0):
        width = value.shape[1]
        gvec_ref[row : row + 1, start : start + width] += value

    def col_sum(value):
        return jnp.sum(value, axis=0, keepdims=True)

    def window_rows(body):
        def one(u, carry):
            body(pl.ds(pl.multiple_of(u * wrows, 8), wrows), u)
            return carry

        for u in range(PAIR):
            one(u, 0)

    def chunks(body):
        body(slice(0, rows_all))

    def stats(x):
        center = x - jnp.mean(x, axis=-1, keepdims=True)
        inv = lax.rsqrt(jnp.mean(center * center, axis=-1, keepdims=True) + NORM_EPS)
        return center * inv, inv

    def load_cells(buf, u):
        return buf[slot, u].astype(F32).reshape(wrows, D)

    def norm_one(rows, u):
        x = load_cells(tokb, u)
        n1, _ = stats(x)
        nm[rows] = (n1 * vec(V_G1) + vec(V_B1)).astype(BF)
        cotw[rows] = load_cells(cotb, u).astype(BF)
        hid[rows] = x

    window_rows(norm_one)

    project = dg(nm[...], wqkv_ref[...], NN)
    for j in range(3):
        part = project[:, j * D : (j + 1) * D]
        if j == 0:
            part = part + vec(V_BQ)
        if j == 2:
            part = part + vec(V_BV)
        for g in range(GROUPS):
            qkv[j * GROUPS + g][:rows_all] = part[:, g * LANES : (g + 1) * LANES]

    UNROLL = 2

    def view(ref, which, u):
        return ref[which].at[pl.ds(pl.multiple_of(u * wrows, 8), KEYS * canv)]

    def take(ref, which, u, c):
        return view(ref, which, u)[pl.ds(c, KEYS, stride=canv)]

    def put(ref, which, u, c, value):
        view(ref, which, u)[pl.ds(c, CELLS, stride=canv)] = value[:CELLS]

    batches = [(u, tuple(range(v, v + UNROLL))) for u in range(PAIR) for v in range(0, canv, UNROLL)]

    def in_turn(*stages):
        held = {}
        for n in range(len(batches) + len(stages) - 1):
            for k, stage in enumerate(stages):
                if 0 <= n - k < len(batches):
                    held[n - k] = stage(*batches[n - k], held.get(n - k))

    def score(u, cs, _):
        raw = {}
        for c in cs:
            for g in range(GROUPS):
                q2 = split_queries(take(qkv, g, u, c))
                k2 = split_keys(take(qkv, GROUPS + g, u, c))
                raw[c, g] = dg(k2, q2, NT)
                q2s[u, c * GROUPS + g] = q2
                k2s[u, c * GROUPS + g] = k2
        return raw

    def soften(u, cs, raw):
        probs = {}
        for c in cs:
            row = lab_ref[u, c : c + 1, :]
            col = jnp.transpose(jnp.broadcast_to(row, (LANES, LANES)))[:KEYS]
            mask = (col == row)[None]
            for g in range(GROUPS):
                s = (raw[c, g] * (SCALE * LOG2E) + bias_ref[g]).reshape(2, KEYS, LANES)
                s = jnp.where(mask, s, -1e30)
                e = jnp.exp2(s - jnp.max(s, axis=1, keepdims=True))
                p = e * (1.0 / jnp.sum(e, axis=1, keepdims=True))
                probs[c, g] = p.reshape(2 * KEYS, LANES).astype(BF)
                prob[u, c * GROUPS + g] = probs[c, g]
        for c in cs[::2]:
            for g in range(GROUPS):
                v2 = [split_keys(take(qkv, 2 * GROUPS + g, u, d)) for d in (c, c + 1)]
                p = jnp.concatenate([probs[c, g], probs[c + 1, g]], axis=0)
                for d in (0, 1):
                    v2s[u, (c + d) * GROUPS + g] = v2[d]
                o = dg(p, corner(*v2), TN)
                put(mix, g, u, c, join_queries(o[:, :LANES]))
                put(mix, g, u, c + 1, join_queries(o[:, LANES:]))

    in_turn(score, soften)

    for g in range(GROUPS):
        mixb[:, g * LANES : (g + 1) * LANES] = mix[g][:rows_all].astype(BF)
    hid[...] += dg(mixb[...], wout_ref[...], NN) + vec(V_BO)

    def norm_two(rows):
        n, inv = stats(hid[rows])
        n2[rows] = n
        inv2[rows] = inv
        nt[rows] = (n * vec(V_G2) + vec(V_B2)).astype(BF)

    chunks(norm_two)

    FC = 768
    for f in range(FF // FC):
        cols = slice(f * FC, (f + 1) * FC)
        up = dg(nt[...], wup_ref[:, cols], NN) + vec_ref[V_BUP : V_BUP + 1, cols]
        dact = dg(cotw[...], wdn_ref[cols, :], NT)
        cdf = 0.5 + 0.5 * lax.erf(up * (0.5**0.5))
        act[:, cols] = (up * cdf).astype(BF)
        slope = cdf + up * (jnp.exp(-0.5 * up * up) * (1.0 / math.sqrt(2.0 * math.pi)))
        gu = (dact * slope).astype(BF)
        gup_act[:, cols] = gu
        add_vec(V_BUP, col_sum(gu.astype(F32)), f * FC)
    hid[...] = hid[...] + dg(act[...], wdn_ref[...], NN) + vec(V_BDN)

    tmp[...] = dg(gup_act[...], wup_ref[...], NT)
    def store_out(rows, u):
        outb[slot, u] = hid[rows].reshape(WIN, WIN, canv, D).astype(BF)

    window_rows(store_out)
    begin(2, out_hbm, outb, step, slot)

    def back_two(rows):
        gn = tmp[rows]
        n = n2[rows]
        c = cotw[rows].astype(F32)
        add_vec(V_G2, col_sum(gn * n))
        add_vec(V_B2, col_sum(gn))
        add_vec(V_BDN, col_sum(c))
        e = gn * vec(V_G2)
        g = c + inv2[rows] * (
            e - jnp.mean(e, axis=-1, keepdims=True) - n * jnp.mean(e * n, axis=-1, keepdims=True)
        )
        ght[rows] = g
        low = g.astype(BF)
        gab[rows] = low
        add_vec(V_BO, col_sum(low.astype(F32)))

    chunks(back_two)
    for f in range(FF // FC):
        cols = slice(f * FC, (f + 1) * FC)
        gup_ref[:, cols] += dg(nt[:main], gup_act[:main, cols], TN)
        gdn_ref[:, cols] += dg(cotw[:main], act[:main, cols], TN)

    part = dg(gab[...], wout_ref[...], NT)
    for g in range(GROUPS):
        tmp3[g][:rows_all] = part[:, g * LANES : (g + 1) * LANES]

    gout_ref[...] += dg(mixb[:main], gab[:main], TN)
    def back_probs(u, cs, _):
        raw, o_of = {}, {}
        for c in cs:
            for g in range(GROUPS):
                v2 = v2s[u, c * GROUPS + g]
                o_of[c, g] = split_queries(take(tmp3, g, u, c))
                raw[c, g] = dg(v2, o_of[c, g], NT)
        return raw, o_of

    def back_rest(u, cs, got):
        raw, o_of = got
        p_of, ds_of = {}, {}

        def side(table, c, g, axis):
            return jnp.concatenate([table[c, g], table[c + 1, g]], axis=axis)

        for c in cs:
            for g in range(GROUPS):
                p_of[c, g] = prob[u, c * GROUPS + g]
                p3 = p_of[c, g].astype(F32).reshape(2, KEYS, LANES)
                dp3 = raw[c, g].reshape(2, KEYS, LANES)
                ds = p3 * (dp3 - jnp.sum(p3 * dp3, axis=1, keepdims=True))
                ds_of[c, g] = ds.reshape(2 * KEYS, LANES).astype(BF)
        for g in range(GROUPS):
            gbias_ref[g] += sum(ds_of[c, g].astype(F32) for c in cs)
        for c in cs[::2]:
            for g in range(GROUPS):
                gv = dg(side(p_of, c, g, 1), corner(o_of[c, g], o_of[c + 1, g]), NN)
                for d in (0, 1):
                    put(dqkv, 2 * GROUPS + g, u, c + d, join_keys(gv[:, d * LANES : (d + 1) * LANES]))
        for c in cs[::2]:
            for g in range(GROUPS):
                q2 = [q2s[u, d * GROUPS + g] for d in (c, c + 1)]
                k2 = [k2s[u, d * GROUPS + g] for d in (c, c + 1)]
                gk = dg(side(ds_of, c, g, 1), corner(*q2), NN)
                gq = dg(side(ds_of, c, g, 0), corner(*k2), TN)
                for d in (0, 1):
                    lanes = slice(d * LANES, (d + 1) * LANES)
                    put(dqkv, g, u, c + d, join_queries(gq[:, lanes]) * SCALE)
                    put(dqkv, GROUPS + g, u, c + d, join_keys(gk[:, lanes]) * SCALE)

    in_turn(back_probs, back_rest)

    def round_back(rows):
        for j in range(3 * GROUPS):
            low = dqkv[j][rows].astype(BF)
            dqb[rows, j * LANES : (j + 1) * LANES] = low
            if j < GROUPS:
                add_vec(V_BQ, col_sum(low.astype(F32)), j * LANES)
            elif j >= 2 * GROUPS:
                add_vec(V_BV, col_sum(low.astype(F32)), (j - 2 * GROUPS) * LANES)

    chunks(round_back)
    tmp[...] = dg(dqb[...], wqkv_ref[...], NT)

    def back_one(rows, u):
        gn = tmp[rows].astype(BF).astype(F32)
        n, inv = stats(load_cells(tokb, u))
        add_vec(V_G1, col_sum(gn * n))
        add_vec(V_B1, col_sum(gn))
        e = gn * vec(V_G1)
        g = ght[rows] + inv * (
            e - jnp.mean(e, axis=-1, keepdims=True) - n * jnp.mean(e * n, axis=-1, keepdims=True)
        )
        gtb[slot, u] = g.reshape(WIN, WIN, canv, D)

    window_rows(back_one)
    gqkv_ref[...] += dg(nm[:main], dqb[:main], TN)
    begin(3, gtok_hbm, gtb, step, slot)
    for key, ref in zip(widths, (nm, mixb, nt, cotw, gab, dqb, act, gup_act)):
        keep(key, ref)

    @pl.when(step + 1 == steps)
    def _():
        gqkv_ref[...] += dg(kept("nm"), kept("dqb"), TN)
        gout_ref[...] += dg(kept("mixb"), kept("gab"), TN)
        gup_ref[...] += dg(kept("nt"), kept("gup"), TN)
        gdn_ref[...] += dg(kept("cotw"), kept("act"), TN)
        for back in (1, 0):
            finish(2, out_hbm, outb, step - back, slot if back == 0 else 1 - slot)
            finish(3, gtok_hbm, gtb, step - back, slot if back == 0 else 1 - slot)
        for ref, base in matrices((gqkv_ref, gout_ref, gup_ref)):
            wide = ref.shape[1] // LANES
            for j in range(wide):
                flat[pl.ds(base + j, D, stride=wide)] = ref[:, j * LANES : (j + 1) * LANES]
        base = D * (3 * D + D + FF) // LANES
        for i in range(FF // LANES):
            for j in range(GROUPS):
                block = gdn_ref[j * LANES : (j + 1) * LANES, i * LANES : (i + 1) * LANES]
                flat[pl.ds(base + i * LANES * GROUPS + j, LANES, stride=GROUPS)] = jnp.transpose(block)
        for row, j, at in vector_rows():
            flat[at : at + 1] = gvec_ref[row : row + 1, j * LANES : (j + 1) * LANES]
        gspread_ref[...] = jnp.zeros_like(gspread_ref)
        for g in range(GROUPS):
            for h in range(2):
                gspread_ref[pl.ds(2 * g + h, KEYS, stride=8)] = gbias_ref[g, h * KEYS : (h + 1) * KEYS]
        size = send_ref.shape[1]
        for k, start in enumerate(starts):
            send_ref[k] = flat[start : start + size].astype(BF)


VECTORS = (D, D, D, FF, D, D, D, D, D)
P_SIZE = D * (3 * D + D + 2 * FF) + sum(VECTORS)


def matrices(refs):
    base, made = 0, []
    for ref in refs:
        made.append((ref, base))
        base += ref.shape[0] * ref.shape[1] // LANES
    return made


def vector_rows():
    at = D * (3 * D + D + 2 * FF) // LANES
    made = []
    for row, width in enumerate(VECTORS):
        for j in range(width // LANES):
            made.append((row, j, at))
            at += 1
    return made


def part_rows(devices):
    return -(-(P_SIZE // devices + LANES - 1) // LANES // 16) * 16


def block_call(tokens, cot, labels, bias, parts):
    canv = tokens.shape[2]
    rows = PAIR * CELLS * canv
    tall = (PAIR - 1) * CELLS * canv + KEYS * canv
    devices, size = parts.shape[:2]
    share = P_SIZE // devices
    starts = tuple(k * share // LANES for k in range(devices))
    flat_rows = -(-max(starts[-1] + size, P_SIZE // LANES) // 8) * 8
    hbm = pl.BlockSpec(memory_space=pl.ANY)

    def whole(*shape):
        return pl.BlockSpec(shape, lambda i: (0,) * len(shape), pipeline_mode=pl.Buffered(1))

    cells = (2, PAIR, WIN, WIN, canv, D)
    return pl.pallas_call(
        partial(block_kernel, canv, starts),
        grid=(BANDS * BANDS // PAIR,),
        out_shape=[
            jax.ShapeDtypeStruct(tokens.shape, BF),
            jax.ShapeDtypeStruct(tokens.shape, F32),
            jax.ShapeDtypeStruct(parts.shape, BF),
            jax.ShapeDtypeStruct((KEYS * 8, LANES), F32),
        ],
        in_specs=[
            hbm, hbm,
            pl.BlockSpec((PAIR, canv, LANES), lambda i: (i, 0, 0)),
            whole(KEYS * 8, LANES),
            hbm,
        ],
        out_specs=[hbm, hbm, whole(*parts.shape), whole(KEYS * 8, LANES)],
        scratch_shapes=[
            pltpu.VMEM((max(flat_rows, 6 * GROUPS * tall), LANES), F32),
            pltpu.VMEM((D, 3 * D), BF),
            pltpu.VMEM((D, D), BF),
            pltpu.VMEM((D, FF), BF),
            pltpu.VMEM((FF, D), BF),
            pltpu.VMEM((16, FF), F32),
            pltpu.VMEM((D, 3 * D), F32),
            pltpu.VMEM((D, D), F32),
            pltpu.VMEM((D, FF), F32),
            pltpu.VMEM((D, FF), F32),
            pltpu.VMEM((16, FF), F32),
            pltpu.SemaphoreType.DMA,
            pltpu.VMEM(cells, BF),
            pltpu.VMEM(cells, BF),
            pltpu.VMEM(cells, BF),
            pltpu.VMEM(cells, F32),
            pltpu.SemaphoreType.DMA((4, 2, 4 * PAIR)),
            pltpu.VMEM((rows, D), BF),
            pltpu.VMEM((rows, D), BF),
            pltpu.VMEM((PAIR, canv * GROUPS, 2 * KEYS, LANES), BF),
            pltpu.VMEM((GROUPS, tall, LANES), F32),
            pltpu.VMEM((rows, D), BF),
            pltpu.VMEM((rows, D), F32),
            pltpu.VMEM((rows, D), BF),
            pltpu.VMEM((rows, D), F32),
            pltpu.VMEM((rows, 1), F32),
            pltpu.VMEM((rows, FF), BF),
            pltpu.VMEM((rows, FF), BF),
            pltpu.VMEM((rows, D), F32),
            pltpu.VMEM((rows, D), BF),
            pltpu.VMEM((rows, 3 * D), BF),
            pltpu.VMEM((rows, D), F32),
            pltpu.VMEM((GROUPS, tall, LANES), F32),
            pltpu.VMEM((BANDS * BANDS // PAIR * (rows % 256), 8 * D + 2 * FF), BF),
            pltpu.VMEM((PAIR, canv * GROUPS, LANES, LANES), BF),
            pltpu.VMEM((PAIR, canv * GROUPS, 2 * KEYS, LANES), BF),
            pltpu.VMEM((PAIR, canv * GROUPS, 2 * KEYS, LANES), BF),
            pltpu.VMEM((GROUPS, 2 * KEYS, LANES), F32),
            pltpu.VMEM((GROUPS, 2 * KEYS, LANES), F32),
        ],
        compiler_params=pltpu.CompilerParams(vmem_limit_bytes=63 << 20),
        name="block",
    )(tokens, cot, labels, bias, parts)


def split_windows(field):
    canvases, band_rows, columns, channels = field.shape
    field = field.reshape(canvases, band_rows // WIN, WIN, columns // WIN, WIN, channels)
    return field.transpose(0, 1, 3, 2, 4, 5).reshape(-1, WIN * WIN, channels)


def window_labels(crop_ids):
    canvases, height, columns = crop_ids.shape
    crop_roll = jnp.roll(crop_ids, (-SHIFT, -SHIFT), (1, 2))
    row_flag = (jnp.arange(height, dtype=jnp.int32) >= height - SHIFT).astype(jnp.int32)
    col_flag = (jnp.arange(columns, dtype=jnp.int32) >= columns - SHIFT).astype(jnp.int32)
    labels = crop_roll * 4 + 2 * row_flag[None, :, None] + col_flag[None, None, :]
    labels = split_windows(labels[..., None])[:, :, 0].reshape(canvases, -1, CELLS)
    labels = jnp.pad(labels, ((0, 0), (0, 0), (0, 64 - CELLS)), constant_values=-1)
    return jnp.concatenate([labels, labels], axis=-1).astype(F32).transpose(1, 0, 2)


def by_pairs(table):
    rows = table.T.reshape(GROUPS, 2, 2, TABLE).transpose(1, 0, 2, 3).reshape(2, 2 * GROUPS, TABLE)
    return jnp.pad(rows, ((0, 0), (0, 2), (0, 176 - TABLE))).reshape(16, 176)


def from_pairs(rows):
    rows = rows[:, :TABLE].reshape(2, 8, TABLE)[:, : 2 * GROUPS].reshape(2, GROUPS, 2, TABLE)
    return rows.transpose(1, 0, 2, 3).reshape(HEADS, TABLE).T


def local_block(tokens, crop_ids, parts, spread, cotangent):
    out_tokens, grad_tokens, send, gspread = block_call(
        tokens.transpose(1, 2, 0, 3), cotangent.transpose(1, 2, 0, 3), window_labels(crop_ids),
        spread.reshape(KEYS * 8, LANES), parts
    )
    return out_tokens.transpose(2, 0, 1, 3), grad_tokens.transpose(2, 0, 1, 3), send, gspread.reshape(KEYS, 8, LANES)


MESH = pl.DeviceIdType.MESH


class Place:
    def __init__(self, sizes):
        self.A, self.Y = sizes[0] // 2, sizes[1] // 2
        dp, shard = lax.axis_index("dp"), lax.axis_index("shard")
        self.a, self.b = dp // 2, lax.rem(dp, 2)
        self.y, self.c = shard // 2, lax.rem(shard, 2)
        self.dp, self.shard = dp, shard

    def at(self, a=None, b=None, y=None, c=None):
        a, b = self.a if a is None else a, self.b if b is None else b
        y, c = self.y if y is None else y, self.c if c is None else c
        return (a * 2 + b, y * 2 + c)

    def turn_a(self, k):
        return lax.rem(self.a + k, self.A)

    def turn_y(self, k):
        return lax.rem(self.y + k, self.Y)

    def peers(self):
        found = [self.at(b=1 - self.b), self.at(c=1 - self.c)]
        found += [self.at(a=self.turn_a(k)) for k in range(1, self.A)]
        found += [self.at(y=self.turn_y(k)) for k in range(1, self.Y)]
        return found


def greet(peers):
    barrier = pltpu.get_barrier_semaphore()
    for peer in peers:
        pl.semaphore_signal(barrier, inc=1, device_id=peer, device_id_type=MESH)
    pl.semaphore_wait(barrier, len(peers))


def offset_hot(rj, cj, width):
    i = lax.rem(lax.broadcasted_iota(jnp.int32, (1, LANES), 1), 64)
    index = (i // WIN) * (2 * WIN - 1) + lax.rem(i, WIN) + TABLE // 2 - (rj * (2 * WIN - 1) + cj)
    index = jnp.where(i < CELLS, index, -1)
    hot = lax.broadcasted_iota(jnp.int32, (width, LANES), 0) == index
    return jnp.where(hot, 1.0, 0.0).astype(BF)


def three_parts(value):
    high = value.astype(BF)
    rest = value - high.astype(F32)
    middle = rest.astype(BF)
    return jnp.concatenate([high, middle, (rest - middle.astype(F32)).astype(BF)], axis=0)


def three_sum(value):
    return value[:16] + value[16:32] + value[32:]


def spread_table(table_ref, bias_ref):
    parts = three_parts(table_ref[...])
    low = lax.broadcasted_iota(jnp.int32, (8, LANES), 1) < 64

    def over(rj, carry):
        for cj in range(WIN):
            got = three_sum(dg(parts, offset_hot(rj, cj, table_ref.shape[1]), NN))
            bias_ref[rj * WIN + cj] = jnp.where(low, got[:8], got[8:])
        return carry

    lax.fori_loop(0, WIN, over, 0)
    bias_ref[CELLS:] = jnp.zeros((KEYS - CELLS, 8, LANES), F32)


def fold_table(bias_ref, width):
    low = lax.broadcasted_iota(jnp.int32, (8, LANES), 1) < 64

    def over(rj, total):
        for cj in range(WIN):
            block = bias_ref[rj * WIN + cj]
            both = jnp.concatenate([jnp.where(low, block, 0.0), jnp.where(low, 0.0, block)], axis=0)
            total = total + dg(three_parts(both), offset_hot(rj, cj, width), NT)
        return total

    return three_sum(lax.fori_loop(0, WIN, over, jnp.zeros((48, width), F32)))


def gather_kernel(sizes, mine, table_ref, all_ref, bias_ref, own_sem, sems):
    me = Place(sizes)
    A, Y = me.A, me.Y
    half = mine.shape[0] // 2
    parts = (pl.ds(0, half), pl.ds(half, half))
    a, b, y, c = me.a, me.b, me.y, me.c
    own = pltpu.make_async_copy(mine, all_ref.at[a, b, y, c], own_sem)
    own.start()
    greet(me.peers())

    def send(kind, k, src, dst, peer):
        copy = pltpu.make_async_remote_copy(
            src_ref=src, dst_ref=dst, send_sem=sems.at[0, kind, k], recv_sem=sems.at[1, kind, k],
            device_id=peer, device_id_type=MESH,
        )
        copy.start()
        return copy

    far = [None]
    for k in range(1, A):
        far.append(send(0, k, mine, all_ref.at[a, b, y, c], me.at(a=lax.rem(a - k + A, A))))
    sent = far[1:]
    ys_peer = [me.at(y=lax.rem(y - j + Y, Y)) for j in range(Y)]
    x_peer, c_peer = me.at(b=1 - b), me.at(c=1 - c)
    state = {}

    def same(kind, k, where, peer):
        return send(kind, k, all_ref.at[where], all_ref.at[where], peer)

    def spread(k):
        if k:
            far[k].wait_recv()
        z = me.turn_a(k)
        lo, hi = (z, b, y, c, parts[0]), (z, b, y, c, parts[1])
        xs = same(1, k, lo, x_peer)
        ys = [same(2, k * Y + j, hi, ys_peer[j]) for j in range(1, Y)]
        more = [same(3, k * Y, hi, x_peer)] + [same(4, k * Y + j, lo, ys_peer[j]) for j in range(1, Y)]
        state[k] = (xs, ys, more)

    def onward(k):
        z = me.turn_a(k)
        xs, ys, more = state[k]
        xs.wait_recv()
        for j in range(1, Y):
            more.append(same(5, k * Y + j, (z, 1 - b, y, c, parts[0]), ys_peer[j]))
        for j in range(1, Y):
            ys[j - 1].wait_recv()
            more.append(same(6, k * Y + j, (z, b, me.turn_y(j), c, parts[1]), x_peer))
        sent.extend([xs] + ys + more)
        state[k] = more

    def across(k):
        z = me.turn_a(k)
        for copy in state[k]:
            copy.wait_recv()
        ends.append(same(7, k, (z, slice(None), slice(None), c), c_peer))

    ends = []
    own.wait()
    for k in range(A + 2):
        if k < A:
            spread(k)
        if k == 0:
            spread_table(table_ref, bias_ref)
        if 0 <= k - 1 < A:
            onward(k - 1)
        if k - 2 >= 0:
            across(k - 2)
    for copy in ends:
        copy.wait_recv()
    for copy in sent + ends:
        copy.wait_send()


def gather_call(mesh_sizes, mine, table):
    A, Y = mesh_sizes[0] // 2, mesh_sizes[1] // 2
    return pl.pallas_call(
        partial(gather_kernel, mesh_sizes),
        out_shape=[
            jax.ShapeDtypeStruct((A, 2, Y, 2) + mine.shape, mine.dtype),
            jax.ShapeDtypeStruct((KEYS, 8, LANES), F32),
        ],
        in_specs=[pl.BlockSpec(memory_space=pltpu.VMEM)] * 2,
        out_specs=[pl.BlockSpec(memory_space=pl.ANY), pl.BlockSpec(memory_space=pltpu.VMEM)],
        scratch_shapes=[pltpu.SemaphoreType.DMA, pltpu.SemaphoreType.DMA((2, 8, A * Y))],
        compiler_params=pltpu.CompilerParams(collective_id=0, has_side_effects=True),
        name="gather",
    )(mine, table)


def scatter_kernel(sizes, share, x_ref, t_ref, sum_ref, tab_ref, norm_ref,
                   b0, y0, bx0, by1, y1h0, y1h1, by0, bx1, y2, bz, tbuf, qbuf, sems, small):
    me = Place(sizes)
    A, Y = me.A, me.Y
    a, b, y, c = me.a, me.b, me.y, me.c
    size = sum_ref.shape[0]
    half = size // 2
    lo, hi = pl.ds(0, half), pl.ds(half, half)
    greet(me.peers())
    sent = []

    def copy_to(table, kind, k, src, dst, peer):
        copy = pltpu.make_async_remote_copy(
            src_ref=src, dst_ref=dst, send_sem=table.at[0, kind, k], recv_sem=table.at[1, kind, k],
            device_id=peer, device_id_type=MESH,
        )
        copy.start()
        sent.append(copy)
        return copy

    send, small_send = partial(copy_to, sems), partial(copy_to, small)
    order = list(range(1, A)) + [0]
    x_peer, c_peer = me.at(b=1 - b), me.at(c=1 - c)
    y_of = [lax.rem(y - j + Y, Y) for j in range(Y)]
    core, first, second, last, tabs = {}, {}, {}, {}, {}
    for k in order:
        core[k] = send(0, k, x_ref.at[me.turn_a(k), :, :, 1 - c], b0.at[k], c_peer)
    tbuf[0] = fold_table(t_ref, tab_ref.shape[1])
    tabs[0] = small_send(0, 0, tbuf.at[0], tbuf.at[1], c_peer)

    def total(*parts):
        out = parts[0].astype(F32)
        for part in parts[1:]:
            out = out + part.astype(F32)
        return out

    def exchange_one(k):
        core[k].wait_recv()
        z = me.turn_a(k)

        def over(i, carry):
            for q in range(Y):
                y0[k, i, q] = total(x_ref[z, i, q, c], b0[k, i, q]).astype(BF)
            return carry

        lax.fori_loop(0, 2, over, 0)
        xs = send(1, k, y0.at[k, 1 - b, :, lo], bx0.at[k], x_peer)
        ys = [send(2, k * Y + j, y0.at[k, :, y_of[j], hi], by1.at[k, j - 1], me.at(y=y_of[j])) for j in range(1, Y)]
        first[k] = (xs, ys)

    def exchange_two(k):
        xs, ys = first[k]
        xs.wait_recv()
        for q in range(Y):
            y1h0[k, q] = total(y0[k, b, q, lo], bx0[k, q]).astype(BF)
        moved = [send(3, k * Y + j, y1h0.at[k, y_of[j]], by0.at[k, j - 1], me.at(y=y_of[j])) for j in range(1, Y)]
        for copy in ys:
            copy.wait_recv()
        for p in range(2):
            y1h1[k, p] = total(y0[k, p, y, hi], *[by1[k, j - 1, p] for j in range(1, Y)]).astype(BF)
        moved.append(send(4, k, y1h1.at[k, 1 - b], bx1.at[k], x_peer))
        second[k] = moved

    def exchange_three(k):
        for copy in second[k]:
            copy.wait_recv()
        low = total(y1h0[k, y], *[by0[k, j - 1] for j in range(1, Y)])
        high = total(y1h1[k, b], bx1[k])
        if k:
            y2[k - 1, lo] = low.astype(BF)
            y2[k - 1, hi] = high.astype(BF)
            last[k] = send(5, k, y2.at[k - 1], bz.at[k - 1], me.at(a=me.turn_a(k)))
        else:
            sum_ref[lo] = low
            sum_ref[hi] = high

    for i in range(A + 2):
        if i < A:
            exchange_one(order[i])
        if i == 0:
            tabs[0].wait_recv()
            tbuf[2] = tbuf[0] + tbuf[1]
            tabs[1] = small_send(1, 0, tbuf.at[2], tbuf.at[3], x_peer)
        if 0 <= i - 1 < A:
            exchange_two(order[i - 1])
        if i == 1:
            tabs[1].wait_recv()
            tbuf[4 + y] = tbuf[2] + tbuf[3]
            tabs[2] = [small_send(2, j, tbuf.at[4 + y], tbuf.at[4 + y], me.at(y=y_of[j])) for j in range(1, Y)]
        if i - 2 >= 0:
            exchange_three(order[i - 2])
        if i == 2:
            for copy in tabs[2]:
                copy.wait_recv()
            tbuf[4 + Y + a] = total(*[tbuf[4 + j] for j in range(Y)])
            tabs[3] = [
                small_send(3, k, tbuf.at[4 + Y + a], tbuf.at[4 + Y + a], me.at(a=lax.rem(a - k + A, A)))
                for k in range(1, A)
            ]
    for k in range(1, A):
        last[k].wait_recv()
    final = total(sum_ref[...], *[bz[k - 1] for k in range(1, A)])
    sum_ref[...] = final
    offset = lax.rem((me.dp * (2 * Y) + me.shard) * share, LANES)
    place = lax.broadcasted_iota(jnp.int32, (size, LANES), 0) * LANES + lax.broadcasted_iota(jnp.int32, (size, LANES), 1)
    live = jnp.logical_and(place >= offset, place < offset + share)
    squares = jnp.where(live, final * final, 0.0).reshape(size // 8, 8, LANES)
    S, G = 2 * Y, 2 * A
    qbuf[me.shard] = jnp.sum(squares, axis=0)
    for copy in [
        small_send(4, k, qbuf.at[me.shard], qbuf.at[me.shard], (me.dp, lax.rem(me.shard - k + S, S))) for k in range(1, S)
    ]:
        copy.wait_recv()
    qbuf[S + me.dp] = total(*[qbuf[k] for k in range(S)])
    round_two = [
        small_send(5, k, qbuf.at[S + me.dp], qbuf.at[S + me.dp], (lax.rem(me.dp - k + G, G), me.shard)) for k in range(1, G)
    ]
    for copy in tabs[3]:
        copy.wait_recv()
    table = total(*[tbuf[4 + Y + k] for k in range(A)])
    tab_ref[...] = table
    table_squares = jnp.sum((table * table).reshape(2, 8, table.shape[1]), axis=0)
    table_squares = table_squares[:, :LANES] + table_squares[:, LANES:]
    for copy in round_two:
        copy.wait_recv()
    both = total(*[qbuf[S + k] for k in range(G)]) + table_squares
    norm = jnp.sqrt(jnp.broadcast_to(jnp.sum(jnp.sum(both, axis=0, keepdims=True), axis=1, keepdims=True), (8, LANES)))
    norm_ref[0:8] = norm
    norm_ref[8:16] = jnp.minimum(1.0, MAX_NORM / (norm + 1e-06))
    for copy in sent:
        copy.wait_send()


def scatter_call(mesh_sizes, share, x, table):
    A, Y = mesh_sizes[0] // 2, mesh_sizes[1] // 2
    size = x.shape[-2]
    half = size // 2
    vmem = pl.BlockSpec(memory_space=pltpu.VMEM)
    widest = max(2 * A, 2 * Y)
    return pl.pallas_call(
        partial(scatter_kernel, mesh_sizes, share),
        out_shape=[
            jax.ShapeDtypeStruct((size, LANES), F32),
            jax.ShapeDtypeStruct((16, 2 * LANES), F32),
            jax.ShapeDtypeStruct((16, LANES), F32),
        ],
        in_specs=[vmem, vmem],
        out_specs=[vmem, vmem, vmem],
        scratch_shapes=[
            pltpu.VMEM((A, 2, Y, size, LANES), BF),
            pltpu.VMEM((A, 2, Y, size, LANES), BF),
            pltpu.VMEM((A, Y, half, LANES), BF),
            pltpu.VMEM((A, Y - 1, 2, half, LANES), BF),
            pltpu.VMEM((A, Y, half, LANES), BF),
            pltpu.VMEM((A, 2, half, LANES), BF),
            pltpu.VMEM((A, Y - 1, half, LANES), BF),
            pltpu.VMEM((A, half, LANES), BF),
            pltpu.VMEM((A - 1, size, LANES), BF),
            pltpu.VMEM((A - 1, size, LANES), BF),
            pltpu.VMEM((4 + Y + A, 16, 2 * LANES), F32),
            pltpu.VMEM((2 * Y + 2 * A, 8, LANES), F32),
            pltpu.SemaphoreType.DMA((2, 6, A * Y)),
            pltpu.SemaphoreType.DMA((2, 6, widest)),
        ],
        compiler_params=pltpu.CompilerParams(
            collective_id=1, has_side_effects=True, vmem_limit_bytes=60 << 20
        ),
        name="scatter",
    )(x, table)


LEARN_RATE = 0.1
BETA_ONE = 0.9
BETA_TWO = 0.999
ADAM_EPS = 1e-08
WEIGHT_DECAY = 0.05
MAX_NORM = 1.0


def adamw(weights, gradient, first_old, second_old):
    first_new = BETA_ONE * first_old + (1.0 - BETA_ONE) * gradient
    second_new = BETA_TWO * second_old + (1.0 - BETA_TWO) * gradient * gradient
    first_hat = first_new / (1.0 - BETA_ONE**STEP)
    second_hat = second_new / (1.0 - BETA_TWO**STEP)
    updated = weights - LEARN_RATE * (first_hat / (jnp.sqrt(second_hat) + ADAM_EPS) + WEIGHT_DECAY * weights)
    return (updated, first_new, second_new)


def local(
    sizes, tokens, crop_ids, params, first_moment, second_moment, bias_table, table_first, table_second, cotangent
):
    devices = sizes[0] * sizes[1]
    share = params.shape[0]
    size = part_rows(devices)
    offset = lax.rem((lax.axis_index("dp") * sizes[1] + lax.axis_index("shard")) * share, LANES)
    wide = jnp.pad(params, (LANES, size * LANES - share))
    mine = lax.dynamic_slice(wide, (LANES - offset,), (size * LANES,))
    parts, spread = gather_call(sizes, mine.reshape(size, LANES).astype(BF), by_pairs(bias_table))
    digits = parts.shape
    out_tokens, grad_tokens, send, gspread = local_block(
        tokens, crop_ids, parts.reshape(devices, size, LANES), spread, cotangent
    )
    total, table_total, norm = scatter_call(sizes, share, send.reshape(digits), gspread)
    grad_shard = lax.dynamic_slice(total.reshape(-1), (offset,), (share,))
    table_grad = from_pairs(table_total)
    grad_norm, factor = norm[0, 0], norm[8, 0]
    new_params, new_first, new_second = adamw(params, grad_shard * factor, first_moment, second_moment)
    new_table, new_table_first, new_table_second = adamw(bias_table, table_grad * factor, table_first, table_second)
    return (
        out_tokens, grad_tokens, grad_shard, table_grad, grad_norm, new_params, new_first, new_second,
        new_table, new_table_first, new_table_second,
    )


def solution(mesh):
    both = P(("dp", "shard"))
    return jax.shard_map(
        partial(local, (mesh.shape["dp"], mesh.shape["shard"])),
        mesh=mesh,
        in_specs=(both, both, both, both, both, P(), P(), P(), both),
        out_specs=(both, both, both, P(), P(), both, both, both, P(), P(), P()),
        check_vma=False,
    )
```
